32 devices in a mesh: context: 8 (over z, x), tensor: 4 (over y, core).
Axes of the slice: x: 2, y: 2, z: 4, core: 2. Of those that a mesh axis runs over, the one named last changes fastest.
Arguments:
- residual_in: float32 [1024, 2048], P(('context', 'tensor')), may hold values from -6 to 6
- grad_output: float32 [1024, 2048], P(('context', 'tensor')), may hold values from -6 to 6
- block_order: int32 [16], replicated, may hold values from 0 to 15, as said below
- w_query: bfloat16 [2, 2048, 2048], P(None, 'context', 'tensor'), may hold values from -0.125 to 0.125
- key_weight: bfloat16 [2, 2048, 1024], P(None, 'context', 'tensor'), may hold values from -0.125 to 0.125
- value_weight: bfloat16 [2, 2048, 1024], P(None, 'context', 'tensor'), may hold values from -0.125 to 0.125
- w_out: bfloat16 [2, 2048, 2048], P(None, 'tensor', 'context'), may hold values from -1.5 to 1.5
- w_gate: bfloat16 [2, 2048, 6144], P(None, 'context', 'tensor'), may hold values from -0.125 to 0.125
- w_up: bfloat16 [2, 2048, 6144], P(None, 'context', 'tensor'), may hold values from -0.125 to 0.125
- w_down: bfloat16 [2, 6144, 2048], P(None, 'tensor', 'context'), may hold values from -0.078125 to 0.078125
- attn_gain: bfloat16 [2, 2048], P(None, 'context'), may hold values from 0.5 to 1.5
- mlp_gain: bfloat16 [2, 2048], P(None, 'context'), may hold values from 0.5 to 1.5
- query_gain: float32 [2, 128], replicated, may hold values from 0.5 to 1.5
- key_gain: float32 [2, 128], replicated, may hold values from 0.5 to 1.5
Outputs:
- final_out: float32 [1024, 2048], P(('context', 'tensor'))
- grad_input: float32 [1024, 2048], P(('context', 'tensor'))
- d_query: float32 [2, 2048, 2048], P(None, 'context', 'tensor')
- d_key: float32 [2, 2048, 1024], P(None, 'context', 'tensor')
- d_value: float32 [2, 2048, 1024], P(None, 'context', 'tensor')
- d_out: float32 [2, 2048, 2048], P(None, 'tensor', 'context')
- d_gate: float32 [2, 2048, 6144], P(None, 'context', 'tensor')
- d_up: float32 [2, 2048, 6144], P(None, 'context', 'tensor')
- d_down: float32 [2, 6144, 2048], P(None, 'tensor', 'context')
- d_attn_gain: float32 [2, 2048], P(None, 'context')
- d_mlp_gain: float32 [2, 2048], P(None, 'context')
- d_query_gain: float32 [2, 128], replicated
- d_key_gain: float32 [2, 128], replicated
The draws below stay inside these ranges and needn't reach their ends.
Inputs may be any that keep to these rules, and one draw needn't show every extreme that they name: `block_order`: a permutation of 0 to 15 in which the entries 2 i and 2 i + 1 always sum to 15.
All inputs are finite; a program needn't handle non-finite values.
Results may differ from the reference program's by a relative error of at most 0.033.
Values may be sent and summed in bfloat16 or wider, within the bound.
No kernel may reach another device: no remote copies, remote signals or barrier semaphores. Data moves between devices by JAX's collectives and lax.ppermute only.
A program may use at most 256 MiB of HBM per device.

```python
import math
import jax
import jax.numpy as jnp
from jax import lax

MODEL_WIDTH = 2048
QUERY_HEADS = 16
KEY_VALUE_HEADS = 8
HEAD_SIZE = 128
FF = 6144
DECODER_LAYERS = 2
BLK = 64
NBLK = 16
SEQUENCE_TOKENS = 1024


def draw_block_order(key, part):
    half_count = NBLK // 2
    order = jax.random.permutation(key, half_count).astype(jnp.int32)
    flips = jax.random.randint(jax.random.fold_in(key, 7), (half_count,), 0, 2)
    leading = jnp.where(flips == 1, NBLK - 1 - order, order)
    trailing = NBLK - 1 - leading
    return jnp.stack([leading, trailing], axis=1).reshape(NBLK).astype(jnp.int32)


def strengthened(entries, stream_key, source, target, blocks, factor):
    owner, partner = [(jnp.arange(entries.shape[dim]) // (entries.shape[dim] // blocks)).reshape([-1 if axis == dim else 1 for axis in range(entries.ndim)]) for dim in (source, target)]
    chosen = jax.random.permutation(stream_key, blocks)[partner]
    strong = (owner == chosen) | (owner == (partner + blocks // 2) % blocks)
    return jnp.where(strong, factor * entries, entries)


def level_of(rng, shape, cuts, low, largest):
    def one(axis_at, shards_of):
        steps = jax.random.uniform(jax.random.fold_in(jax.random.fold_in(rng, 6), axis_at), (shards_of,), jnp.float32, low / len(cuts), largest / len(cuts))
        return jnp.repeat(jnp.exp(steps), shape[axis_at] // shards_of).reshape((-1,) + (1,) * (len(shape) - axis_at - 1))

    gain = one(*cuts[0])
    for cut in cuts[1:]:
        gain = gain * one(*cut)
    return gain


def scatter_about(own_key, dims, width, limit, shards=(), kind=jnp.bfloat16):
    gain = level_of(own_key, dims, shards, -0.22, 0.18) if shards else 1.0
    drawn = jax.random.normal(own_key, dims, jnp.float32) * width * gain
    return jnp.minimum(jnp.maximum(drawn, -limit), limit).astype(kind)


def bell_draw_with(own_key, extent, deviation, most, split, heavy, kind=jnp.bfloat16):
    entries = deviation * jax.random.normal(own_key, extent, jnp.float32)
    if split:
        entries = entries * level_of(own_key, extent, split, -0.22, 0.18)
    return jnp.clip(strengthened(entries, jax.random.fold_in(own_key, 3), *heavy), -most, most).astype(kind)


def setup_inputs(seed: int = 0) -> dict:
    key_of = jax.random.split(jax.random.key(seed), 15)
    residual_in = bell_draw_with(key_of[0], (SEQUENCE_TOKENS, MODEL_WIDTH), 1.0, 6.0, ((0, 32),), (0, 1, 32, 2.75), jnp.float32)
    grad_output = bell_draw_with(key_of[1], (SEQUENCE_TOKENS, MODEL_WIDTH), 1.0, 6.0, ((0, 32),), (0, 1, 32, 2.75), jnp.float32)
    block_order = draw_block_order(jax.random.fold_in(key_of[14], 71), 0)
    w_query = scatter_about(key_of[3], (DECODER_LAYERS, MODEL_WIDTH, QUERY_HEADS * HEAD_SIZE), MODEL_WIDTH ** -0.5, 0.125, ((1, 8), (2, 4)))
    key_weight = scatter_about(key_of[4], (DECODER_LAYERS, MODEL_WIDTH, KEY_VALUE_HEADS * HEAD_SIZE), MODEL_WIDTH ** -0.5, 0.125, ((1, 8), (2, 4)))
    value_weight = scatter_about(key_of[5], (DECODER_LAYERS, MODEL_WIDTH, KEY_VALUE_HEADS * HEAD_SIZE), MODEL_WIDTH ** -0.5, 0.125, ((1, 8), (2, 4)))
    w_out = scatter_about(key_of[6], (DECODER_LAYERS, QUERY_HEADS * HEAD_SIZE, MODEL_WIDTH), (HEAD_SIZE // 8) ** -0.5, 1.5, ((1, 4), (2, 8)))
    w_gate = scatter_about(key_of[7], (DECODER_LAYERS, MODEL_WIDTH, FF), MODEL_WIDTH ** -0.5, 0.125, ((1, 8), (2, 4)))
    w_up = scatter_about(key_of[8], (DECODER_LAYERS, MODEL_WIDTH, FF), MODEL_WIDTH ** -0.5, 0.125, ((1, 8), (2, 4)))
    w_down = scatter_about(key_of[9], (DECODER_LAYERS, FF, MODEL_WIDTH), FF ** -0.5, 0.078125, ((1, 4), (2, 8)))
    attn_gain = jnp.clip(1.0 + 0.1 * jax.random.normal(key_of[10], (DECODER_LAYERS, MODEL_WIDTH), jnp.float32), 0.5, 1.5).astype(jnp.bfloat16)
    mlp_gain = jnp.clip(1.0 + 0.1 * jax.random.normal(key_of[11], (DECODER_LAYERS, MODEL_WIDTH), jnp.float32), 0.5, 1.5).astype(jnp.bfloat16)
    query_gain = jnp.clip(1.0 + 0.1 * jax.random.normal(key_of[12], (DECODER_LAYERS, HEAD_SIZE), jnp.float32), 0.5, 1.5)
    key_gain = jnp.clip(1.0 + 0.1 * jax.random.normal(key_of[13], (DECODER_LAYERS, HEAD_SIZE), jnp.float32), 0.5, 1.5)
    return dict(residual_in=residual_in, grad_output=grad_output, block_order=block_order, w_query=w_query, key_weight=key_weight, value_weight=value_weight, w_out=w_out, w_gate=w_gate, w_up=w_up, w_down=w_down, attn_gain=attn_gain, mlp_gain=mlp_gain, query_gain=query_gain, key_gain=key_gain)


EPSILON = 1e-06
THETA = 1000000.0

def rms_scale(row_data, gain_row):
    mean_square = lax.optimization_barrier(jnp.mean(row_data * row_data, axis=-1, keepdims=True))
    return row_data * lax.rsqrt(mean_square + EPSILON) * gain_row

def rotary_tables(positions):
    half_dim = HEAD_SIZE // 2
    exponent = jnp.arange(half_dim, dtype=jnp.float32) * (2.0 / HEAD_SIZE)
    inverse = jnp.power(jnp.float32(THETA), -exponent)
    angles = positions.astype(jnp.float32)[:, None] * inverse[None, :]
    return (jnp.cos(angles), jnp.sin(angles))

def head_prep(projected, gain_row, cosine, sine_table):
    normed = rms_scale(projected, gain_row)
    half_dim = HEAD_SIZE // 2
    leading = normed[..., :half_dim]
    trailing = normed[..., half_dim:]
    cos_rows = cosine[:, None, :]
    sin_rows = sine_table[:, None, :]
    return jnp.concatenate([leading * cos_rows - trailing * sin_rows, trailing * cos_rows + leading * sin_rows], axis=-1)

def attend_forward(query_rows, key_rows, value_rows, positions):
    rows_per_block = math.gcd(SEQUENCE_TOKENS, 512)
    head_groups = QUERY_HEADS // KEY_VALUE_HEADS
    score_scale = HEAD_SIZE ** (-0.5)
    key_data = key_rows.astype(jnp.float32)
    value_data = value_rows.astype(jnp.float32)
    blocks_of_query = query_rows.reshape(SEQUENCE_TOKENS // rows_per_block, rows_per_block, KEY_VALUE_HEADS, head_groups, HEAD_SIZE)
    position_blocks = positions.reshape(SEQUENCE_TOKENS // rows_per_block, rows_per_block)

    def one_block(block_pair):
        query_block, query_pos = block_pair
        scores = jnp.einsum('qkgd,tkd->kgqt', query_block.astype(jnp.float32), key_data) * score_scale
        causal = positions[None, :] <= query_pos[:, None]
        weights = jnp.where(causal, jnp.exp(scores), 0.0)
        totals = lax.optimization_barrier(jnp.sum(weights, axis=-1))
        rounded = lax.optimization_barrier(weights.astype(jnp.bfloat16)).astype(jnp.float32)
        summed = jnp.einsum('kgqt,tkd->qkgd', rounded, value_data)
        output_block = summed / jnp.transpose(totals, (2, 0, 1))[..., None]
        return (output_block.astype(jnp.bfloat16), jnp.log(totals))
    output_rows, log_totals = lax.map(one_block, (blocks_of_query, position_blocks))
    return (output_rows.reshape(SEQUENCE_TOKENS, QUERY_HEADS * HEAD_SIZE), log_totals)

def attend_backward(query_rows, key_rows, value_rows, positions, output_rows, log_totals, attention_gradient):
    rows_per_block = math.gcd(SEQUENCE_TOKENS, 512)
    head_groups = QUERY_HEADS // KEY_VALUE_HEADS
    score_scale = HEAD_SIZE ** (-0.5)
    key_data = key_rows.astype(jnp.float32)
    value_data = value_rows.astype(jnp.float32)
    count_of_blocks = SEQUENCE_TOKENS // rows_per_block
    delta_terms = lax.optimization_barrier(jnp.sum((attention_gradient.astype(jnp.float32) * output_rows.astype(jnp.float32)).reshape(SEQUENCE_TOKENS, KEY_VALUE_HEADS, head_groups, HEAD_SIZE), axis=-1))
    blocks_of_query = query_rows.reshape(count_of_blocks, rows_per_block, KEY_VALUE_HEADS, head_groups, HEAD_SIZE)
    gradient_blocks = attention_gradient.reshape(count_of_blocks, rows_per_block, KEY_VALUE_HEADS, head_groups, HEAD_SIZE)
    blocks_of_delta = delta_terms.reshape(count_of_blocks, rows_per_block, KEY_VALUE_HEADS, head_groups)
    position_blocks = positions.reshape(count_of_blocks, rows_per_block)

    def one_block(state_pair, block_in):
        key_grad, value_gradient = state_pair
        query_block, query_pos, grad_block, delta_block, log_block = block_in
        query_data = query_block.astype(jnp.float32)
        grad_data = grad_block.astype(jnp.float32)
        scores = jnp.einsum('qkgd,tkd->kgqt', query_data, key_data) * score_scale
        causal = positions[None, :] <= query_pos[:, None]
        probs_full = jnp.where(causal, jnp.exp(scores - log_block[..., None]), 0.0)
        rounded = lax.optimization_barrier(probs_full.astype(jnp.bfloat16)).astype(jnp.float32)
        value_gradient = value_gradient + jnp.einsum('kgqt,qkgd->tkd', rounded, grad_data)
        grad_probs = jnp.einsum('qkgd,tkd->kgqt', grad_data, value_data)
        delta_cols = jnp.transpose(delta_block, (1, 2, 0))[..., None]
        grad_scores = probs_full * (grad_probs - delta_cols) * score_scale
        grad_scores = lax.optimization_barrier(grad_scores.astype(jnp.bfloat16)).astype(jnp.float32)
        query_grad = jnp.einsum('kgqt,tkd->qkgd', grad_scores, key_data)
        key_grad = key_grad + jnp.einsum('kgqt,qkgd->tkd', grad_scores, query_data)
        return ((key_grad, value_gradient), query_grad)
    zero_key_value = jnp.zeros((SEQUENCE_TOKENS, KEY_VALUE_HEADS, HEAD_SIZE), jnp.float32)
    (key_grad, value_gradient), query_grad = lax.scan(one_block, (zero_key_value, zero_key_value), (blocks_of_query, position_blocks, gradient_blocks, blocks_of_delta, log_totals))
    return (query_grad.reshape(SEQUENCE_TOKENS, QUERY_HEADS, HEAD_SIZE), key_grad, value_gradient)

def reference(residual_in, grad_output, block_order, w_query, key_weight, value_weight, w_out, w_gate, w_up, w_down, attn_gain, mlp_gain, query_gain, key_gain):
    positions = jnp.repeat(block_order, BLK) * BLK + jnp.tile(jnp.arange(BLK, dtype=jnp.int32), NBLK)
    cosine, sine_table = rotary_tables(positions)
    current = residual_in
    saved_layers = []
    for layer_index in range(DECODER_LAYERS):
        gain_attn = attn_gain[layer_index].astype(jnp.float32)
        gain_mlp = mlp_gain[layer_index].astype(jnp.float32)
        normalized_input = rms_scale(current, gain_attn).astype(jnp.bfloat16)
        query_proj = jnp.dot(normalized_input, w_query[layer_index], preferred_element_type=jnp.float32).reshape(SEQUENCE_TOKENS, QUERY_HEADS, HEAD_SIZE)
        key_projected = jnp.dot(normalized_input, key_weight[layer_index], preferred_element_type=jnp.float32).reshape(SEQUENCE_TOKENS, KEY_VALUE_HEADS, HEAD_SIZE)
        value_projected = jnp.dot(normalized_input, value_weight[layer_index], preferred_element_type=jnp.float32).reshape(SEQUENCE_TOKENS, KEY_VALUE_HEADS, HEAD_SIZE)
        query_rows = head_prep(query_proj, query_gain[layer_index], cosine, sine_table).astype(jnp.bfloat16)
        key_rows = head_prep(key_projected, key_gain[layer_index], cosine, sine_table).astype(jnp.bfloat16)
        value_rows = value_projected.astype(jnp.bfloat16)
        output_rows, log_totals = attend_forward(query_rows, key_rows, value_rows, positions)
        middle = current + jnp.dot(output_rows, w_out[layer_index], preferred_element_type=jnp.float32)
        normed_mid = rms_scale(middle, gain_mlp).astype(jnp.bfloat16)
        gate_proj = jnp.dot(normed_mid, w_gate[layer_index], preferred_element_type=jnp.float32)
        up_proj = jnp.dot(normed_mid, w_up[layer_index], preferred_element_type=jnp.float32)
        hidden = (jax.nn.silu(gate_proj) * up_proj).astype(jnp.bfloat16)
        saved_layers.append((current, normalized_input, query_proj, key_projected, query_rows, key_rows, value_rows, output_rows, log_totals, middle, normed_mid, gate_proj, up_proj, hidden))
        current = middle + jnp.dot(hidden, w_down[layer_index], preferred_element_type=jnp.float32)
    final_out = current
    grad_res = grad_output
    grads_by_layer = []
    for layer_index in reversed(range(DECODER_LAYERS)):
        layer_in, normalized_input, query_proj, key_projected, query_rows, key_rows, value_rows, output_rows, log_totals, middle, normed_mid, gate_proj, up_proj, hidden = saved_layers[layer_index]
        gain_attn = attn_gain[layer_index].astype(jnp.float32)
        gain_mlp = mlp_gain[layer_index].astype(jnp.float32)
        grad_bf = grad_res.astype(jnp.bfloat16)
        d_down = jnp.dot(hidden.T, grad_bf, preferred_element_type=jnp.float32)
        grad_hidden = jnp.dot(grad_bf, w_down[layer_index].T, preferred_element_type=jnp.float32)
        sigmoid_gate = jax.nn.sigmoid(gate_proj)
        grad_up = (grad_hidden * gate_proj * sigmoid_gate).astype(jnp.bfloat16)
        grad_gate = (grad_hidden * up_proj * sigmoid_gate * (1.0 + gate_proj * (1.0 - sigmoid_gate))).astype(jnp.bfloat16)
        d_gate = jnp.dot(normed_mid.T, grad_gate, preferred_element_type=jnp.float32)
        d_up = jnp.dot(normed_mid.T, grad_up, preferred_element_type=jnp.float32)
        grad_normed_mid = jnp.dot(grad_gate, w_gate[layer_index].T, preferred_element_type=jnp.float32) + jnp.dot(grad_up, w_up[layer_index].T, preferred_element_type=jnp.float32)
        unused, norm_back = jax.vjp(rms_scale, middle, gain_mlp)
        grad_mid_part, d_mlp_gain = norm_back(grad_normed_mid)
        grad_mid = grad_res + grad_mid_part
        grad_mid_bf = grad_mid.astype(jnp.bfloat16)
        d_out = jnp.dot(output_rows.T, grad_mid_bf, preferred_element_type=jnp.float32)
        attention_gradient = jnp.dot(grad_mid_bf, w_out[layer_index].T, preferred_element_type=jnp.float32).astype(jnp.bfloat16)
        query_grad, key_grad, value_gradient = attend_backward(query_rows, key_rows, value_rows, positions, output_rows, log_totals, attention_gradient)
        unused, query_back = jax.vjp(lambda projected, gain_row: head_prep(projected, gain_row, cosine, sine_table), query_proj, query_gain[layer_index])
        grad_qproj, d_query_gain = query_back(query_grad)
        unused, key_back = jax.vjp(lambda projected, gain_row: head_prep(projected, gain_row, cosine, sine_table), key_projected, key_gain[layer_index])
        key_projection_gradient, d_key_gain = key_back(key_grad)
        grad_q_bf = grad_qproj.reshape(SEQUENCE_TOKENS, QUERY_HEADS * HEAD_SIZE).astype(jnp.bfloat16)
        key_gradient_narrow = key_projection_gradient.reshape(SEQUENCE_TOKENS, KEY_VALUE_HEADS * HEAD_SIZE).astype(jnp.bfloat16)
        value_gradient_narrow = value_gradient.reshape(SEQUENCE_TOKENS, KEY_VALUE_HEADS * HEAD_SIZE).astype(jnp.bfloat16)
        d_query = jnp.dot(normalized_input.T, grad_q_bf, preferred_element_type=jnp.float32)
        d_key = jnp.dot(normalized_input.T, key_gradient_narrow, preferred_element_type=jnp.float32)
        d_value = jnp.dot(normalized_input.T, value_gradient_narrow, preferred_element_type=jnp.float32)
        grad_normed_in = jnp.dot(grad_q_bf, w_query[layer_index].T, preferred_element_type=jnp.float32)
        grad_normed_in = grad_normed_in + jnp.dot(key_gradient_narrow, key_weight[layer_index].T, preferred_element_type=jnp.float32)
        grad_normed_in = grad_normed_in + jnp.dot(value_gradient_narrow, value_weight[layer_index].T, preferred_element_type=jnp.float32)
        unused, input_back = jax.vjp(rms_scale, layer_in, gain_attn)
        grad_in_part, d_attn_gain = input_back(grad_normed_in)
        grad_res = grad_mid + grad_in_part
        grads_by_layer.append((d_query, d_key, d_value, d_out, d_gate, d_up, d_down, d_attn_gain, d_mlp_gain, d_query_gain, d_key_gain))
    grads_by_layer = grads_by_layer[::-1]
    stacked = tuple((jnp.stack([grads_by_layer[layer_index][member] for layer_index in range(DECODER_LAYERS)]) for member in range(11)))
    return (final_out, grad_res, stacked[0], stacked[1], stacked[2], stacked[3], stacked[4], stacked[5], stacked[6], stacked[7], stacked[8], stacked[9], stacked[10])
```

```python
import jax
import jax.numpy as jnp
from jax import lax
from jax.sharding import PartitionSpec as P

EPSILON = 1e-06
THETA = 1000000.0
AXES = ("context", "tensor")
BF = jnp.bfloat16
F32 = jnp.float32


def mm(a, b):
    return jnp.dot(a, b, preferred_element_type=F32)


def mm_tn(a, b):
    return lax.dot_general(a, b, (((0,), (0,)), ((), ())), preferred_element_type=F32)


def mm_nt(a, b):
    return lax.dot_general(a, b, (((1,), (1,)), ((), ())), preferred_element_type=F32)


def rms_scale(row_data, gain_row):
    mean_square = jnp.mean(row_data * row_data, axis=-1, keepdims=True)
    return row_data * lax.rsqrt(mean_square + EPSILON) * gain_row


def rotary_tables(positions, head_dim):
    half_dim = head_dim // 2
    exponent = jnp.arange(half_dim, dtype=F32) * (2.0 / head_dim)
    inverse = jnp.power(F32(THETA), -exponent)
    angles = positions.astype(F32)[:, None] * inverse[None, :]
    return (jnp.cos(angles), jnp.sin(angles))


def head_prep(projected, gain_row, cosine, sine_table):
    normed = rms_scale(projected, gain_row)
    half_dim = projected.shape[-1] // 2
    leading = normed[..., :half_dim]
    trailing = normed[..., half_dim:]
    cos_rows = cosine[:, None, :]
    sin_rows = sine_table[:, None, :]
    return jnp.concatenate(
        [leading * cos_rows - trailing * sin_rows, trailing * cos_rows + leading * sin_rows],
        axis=-1,
    )


def row_positions(block_order, first_row, row_count, rows_per_block):
    rows_index = first_row + jnp.arange(row_count, dtype=jnp.int32)
    slot_index = rows_index // rows_per_block
    slots = jnp.arange(block_order.shape[0], dtype=jnp.int32)
    matches = slot_index[:, None] == slots[None, :]
    owners = jnp.sum(jnp.where(matches, block_order[None, :], 0), axis=1)
    return owners * rows_per_block + rows_index % rows_per_block


class Links:
    def __init__(self, contexts, tensors):
        self.contexts, self.tensors = contexts, tensors
        high, rows = contexts // 2, tensors // 2

        def at(z, x, y, core):
            return (z * 2 + x) * tensors + y * 2 + core

        self.high = high
        self.square = 2 * rows
        self.line_groups = [
            [at(z, x, y, core) for z in range(high)]
            for x in range(2)
            for y in range(rows)
            for core in range(2)
        ]
        self.square_groups = [
            [at(z, x, y, core) for x in range(2) for y in range(rows)]
            for z in range(high)
            for core in range(2)
        ]
        self.pair = [(i, i ^ 1) for i in range(contexts * tensors)]

    def swap_pair(self, value):
        return lax.ppermute(value, AXES, self.pair)

    def exchange(self, chunks, groups):
        return lax.all_to_all(chunks, AXES, 0, 0, axis_index_groups=groups)

    def spread(self, value, groups):
        count = len(groups[0])
        return self.exchange(jnp.broadcast_to(value[None], (count, *value.shape)), groups)

    def exchange_context(self, chunks):
        return lax.all_to_all(chunks, "context", 0, 0)

    def spread_context(self, value):
        return self.exchange_context(
            jnp.broadcast_to(value[None], (self.contexts, *value.shape))
        )

    def gather_rows(self, rows):
        width = rows.shape[1]
        line = self.spread(rows, self.line_groups).reshape(-1, width)
        own = self.spread(line, self.square_groups).reshape(-1, width)
        return own, self.swap_pair(own)

    def reduce_rows(self, own, other):
        width = own.shape[1]
        half = own + self.swap_pair(other.astype(BF)).astype(F32)
        half = half.astype(BF).reshape(self.square, -1, width)
        quarter = jnp.sum(self.exchange(half, self.square_groups).astype(F32), axis=0)
        quarter = quarter.astype(BF).reshape(self.high, -1, width)
        return jnp.sum(self.exchange(quarter, self.line_groups).astype(F32), axis=0)

    def columns(self, rows):
        count, width = rows.shape
        pieces = rows.reshape(count, self.contexts, width // self.contexts).transpose(1, 0, 2)
        return self.exchange_context(pieces).reshape(count * self.contexts, -1)


def body(
    residual_in,
    grad_output,
    block_order,
    w_query,
    key_weight,
    value_weight,
    w_out,
    w_gate,
    w_up,
    w_down,
    attn_gain,
    mlp_gain,
    query_gain,
    key_gain,
):
    contexts, tensors = lax.axis_size("context"), lax.axis_size("tensor")
    links = Links(contexts, tensors)
    layers = w_query.shape[0]
    head_dim = query_gain.shape[1]
    local_rows, width = residual_in.shape
    context_rows = local_rows * tensors
    rows_per_block = context_rows // 2
    all_rows = context_rows * contexts
    context_pos = lax.axis_index("context")
    query_pos = row_positions(block_order, context_pos * context_rows, context_rows, rows_per_block)
    key_pos = row_positions(block_order, jnp.int32(0), all_rows, rows_per_block)
    causal = key_pos[None, :] <= query_pos[:, None]
    cosine, sine_table = rotary_tables(query_pos, head_dim)
    query_width, kv_width = w_query.shape[2], key_weight.shape[2]
    query_heads = query_width // head_dim
    kv_heads = kv_width // head_dim
    head_groups = query_heads // kv_heads
    score_scale = head_dim ** (-0.5)
    units = w_gate.shape[2] // contexts
    shard = w_query.shape[1]

    with jax.named_scope("gains"):
        gains = jnp.concatenate([attn_gain, mlp_gain], axis=0)
        gains = links.spread_context(gains).transpose(1, 0, 2).reshape(2 * layers, width)
        gains = gains.astype(F32)

    def spread_rows(rows):
        return lax.all_gather(rows, "tensor", axis=0, tiled=True)

    def sum_rows(partial):
        pieces = partial.astype(BF).reshape(tensors, local_rows, width)
        return jnp.sum(lax.all_to_all(pieces, "tensor", 0, 0).astype(F32), axis=0)

    attn_weights, out_weights, ffn_in, ffn_out = [], [], [], []
    for layer in range(layers):
        with jax.named_scope(f"weights_{layer}"):
            packed = jnp.concatenate(
                [w_query[layer], key_weight[layer], value_weight[layer]], axis=1
            )
            attn_weights.append(lax.all_gather(packed, "context", axis=0, tiled=True))
            out_weights.append(lax.all_gather(w_out[layer], "context", axis=1, tiled=True))
            pieces = jnp.concatenate(
                [
                    w_gate[layer].reshape(shard, contexts, units),
                    w_up[layer].reshape(shard, contexts, units),
                ],
                axis=2,
            ).transpose(1, 0, 2)
            ffn_in.append(links.exchange_context(pieces).reshape(width, 2 * units))
            pieces = w_down[layer].reshape(contexts, units, shard)
            ffn_out.append(
                links.exchange_context(pieces).transpose(1, 0, 2).reshape(units, width)
            )

    current = residual_in
    stored = []
    for layer in range(layers):
        gain_attn, gain_mlp = gains[layer], gains[layers + layer]
        with jax.named_scope(f"fwd_{layer}_attn"):
            normed_in = spread_rows(rms_scale(current, gain_attn).astype(BF))
            projected = mm(normed_in, attn_weights[layer])
            query_proj = projected[:, :query_width].reshape(context_rows, query_heads, head_dim)
            key_proj = projected[:, query_width : query_width + kv_width].reshape(
                context_rows, kv_heads, head_dim
            )
            value_rows = projected[:, query_width + kv_width :].astype(BF)
            query_rows = head_prep(query_proj, query_gain[layer], cosine, sine_table).astype(BF)
            key_rows = (
                head_prep(key_proj, key_gain[layer], cosine, sine_table)
                .astype(BF)
                .reshape(context_rows, kv_width)
            )
            pairs = links.spread_context(jnp.concatenate([key_rows, value_rows], axis=1))
            pairs = pairs.reshape(all_rows, 2 * kv_width)
            keys = pairs[:, :kv_width].reshape(all_rows, kv_heads, head_dim)
            values = pairs[:, kv_width:].reshape(all_rows, kv_heads, head_dim)
            grouped = query_rows.reshape(context_rows, kv_heads, head_groups, head_dim)
            scores = (
                jnp.einsum("qkgd,tkd->kgqt", grouped, keys, preferred_element_type=F32)
                * score_scale
            )
            weights = jnp.where(causal, jnp.exp(scores), 0.0)
            totals = jnp.sum(weights, axis=-1)
            summed = jnp.einsum(
                "kgqt,tkd->kgqd", weights.astype(BF), values, preferred_element_type=F32
            )
            output_rows = (
                jnp.transpose(summed / totals[..., None], (2, 0, 1, 3))
                .reshape(context_rows, query_width)
                .astype(BF)
            )
            log_totals = jnp.log(totals)
            middle = current + sum_rows(mm(output_rows, out_weights[layer]))
        with jax.named_scope(f"fwd_{layer}_side"):
            input_columns = links.columns(normed_in)
            output_all = links.spread_context(output_rows).reshape(all_rows, query_width)
        with jax.named_scope(f"fwd_{layer}_ffn"):
            normed_mid = links.gather_rows(rms_scale(middle, gain_mlp).astype(BF))
            inner, partial = [], []
            for rows in normed_mid:
                both = mm(rows, ffn_in[layer])
                gate, up = both[:, :units], both[:, units:]
                hidden = (jax.nn.silu(gate) * up).astype(BF)
                inner.append((gate, up, hidden))
                partial.append(mm(hidden, ffn_out[layer]))
            block_out = middle + links.reduce_rows(*partial)
        stored.append(
            (
                current,
                input_columns,
                query_proj,
                key_proj,
                grouped,
                keys,
                values,
                output_rows,
                output_all,
                log_totals,
                middle,
                normed_mid,
                inner,
            )
        )
        current = block_out

    grad_res = grad_output
    weight_grads, gain_grads = [None] * layers, [None] * layers
    for layer in reversed(range(layers)):
        (
            layer_in,
            input_columns,
            query_proj,
            key_proj,
            grouped,
            keys,
            values,
            output_rows,
            output_all,
            log_totals,
            middle,
            normed_mid,
            inner,
        ) = stored[layer]
        gain_attn, gain_mlp = gains[layer], gains[layers + layer]
        with jax.named_scope(f"bwd_{layer}_ffn"):
            grad_all = links.gather_rows(grad_res.astype(BF))
            partial, d_in, d_down = [], 0.0, 0.0
            for rows, grad_rows, (gate, up, hidden) in zip(normed_mid, grad_all, inner):
                grad_hidden = mm_nt(grad_rows, ffn_out[layer])
                sigmoid = jax.nn.sigmoid(gate)
                grad_up = (grad_hidden * gate * sigmoid).astype(BF)
                grad_gate = (
                    grad_hidden * up * sigmoid * (1.0 + gate * (1.0 - sigmoid))
                ).astype(BF)
                both = jnp.concatenate([grad_gate, grad_up], axis=1)
                partial.append(mm_nt(both, ffn_in[layer]))
                d_in = d_in + mm_tn(rows, both)
                d_down = d_down + mm_tn(hidden, grad_rows)
            grad_normed_mid = links.reduce_rows(*partial)
            unused, norm_back = jax.vjp(rms_scale, middle, gain_mlp)
            grad_mid_part, d_mlp_gain = norm_back(grad_normed_mid)
            grad_mid = grad_res + grad_mid_part
        with jax.named_scope(f"bwd_{layer}_ffn_weights"):
            pieces = links.exchange_context(d_in.astype(BF).reshape(contexts, shard, 2 * units))
            pieces = pieces.transpose(1, 0, 2).astype(F32)
            d_gate = pieces[:, :, :units].reshape(shard, contexts * units)
            d_up = pieces[:, :, units:].reshape(shard, contexts * units)
            pieces = d_down.astype(BF).reshape(units, contexts, shard).transpose(1, 0, 2)
            d_down = links.exchange_context(pieces).reshape(contexts * units, shard).astype(F32)
        with jax.named_scope(f"bwd_{layer}_attn"):
            grad_mid_all = spread_rows(grad_mid.astype(BF))
            grad_columns = links.columns(grad_mid_all)
            d_out = mm_tn(output_all, grad_columns)
            attention_gradient = mm_nt(grad_mid_all, out_weights[layer]).astype(BF)
            grad_grouped = attention_gradient.reshape(context_rows, kv_heads, head_groups, head_dim)
            deltas = jnp.sum(
                (attention_gradient.astype(F32) * output_rows.astype(F32)).reshape(
                    context_rows, kv_heads, head_groups, head_dim
                ),
                axis=-1,
            )
            deltas = jnp.transpose(deltas, (1, 2, 0))[..., None]
            scores = (
                jnp.einsum("qkgd,tkd->kgqt", grouped, keys, preferred_element_type=F32)
                * score_scale
            )
            probs = jnp.where(causal, jnp.exp(scores - log_totals[..., None]), 0.0)
            value_grad = jnp.einsum(
                "kgqt,qkgd->tkd", probs.astype(BF), grad_grouped, preferred_element_type=F32
            )
            grad_probs = jnp.einsum(
                "qkgd,tkd->kgqt", grad_grouped, values, preferred_element_type=F32
            )
            grad_scores = (probs * (grad_probs - deltas) * score_scale).astype(BF)
            query_grad = jnp.einsum(
                "kgqt,tkd->qkgd", grad_scores, keys, preferred_element_type=F32
            ).reshape(context_rows, query_heads, head_dim)
            key_grad = jnp.einsum(
                "kgqt,qkgd->tkd", grad_scores, grouped, preferred_element_type=F32
            )
            pair_grads = jnp.concatenate(
                [
                    key_grad.reshape(contexts, context_rows, kv_width),
                    value_grad.reshape(contexts, context_rows, kv_width),
                ],
                axis=2,
            ).astype(BF)
            pair_sums = jnp.sum(links.exchange_context(pair_grads).astype(F32), axis=0)
            key_grad = pair_sums[:, :kv_width].reshape(context_rows, kv_heads, head_dim)
            value_grad = pair_sums[:, kv_width:]

            def prep(projected, gain_row):
                return head_prep(projected, gain_row, cosine, sine_table)

            unused, query_back = jax.vjp(prep, query_proj, query_gain[layer])
            grad_qproj, d_query_gain = query_back(query_grad)
            unused, key_back = jax.vjp(prep, key_proj, key_gain[layer])
            grad_kproj, d_key_gain = key_back(key_grad)
            grad_projected = jnp.concatenate(
                [
                    grad_qproj.reshape(context_rows, query_width),
                    grad_kproj.reshape(context_rows, kv_width),
                    value_grad,
                ],
                axis=1,
            ).astype(BF)
            grad_normed_in = sum_rows(mm_nt(grad_projected, attn_weights[layer]))
            unused, input_back = jax.vjp(rms_scale, layer_in, gain_attn)
            grad_in_part, d_attn_gain = input_back(grad_normed_in)
            grad_res = grad_mid + grad_in_part
        with jax.named_scope(f"bwd_{layer}_attn_weights"):
            grad_projected_all = links.spread_context(grad_projected).reshape(all_rows, -1)
            d_projected = mm_tn(input_columns, grad_projected_all)
        weight_grads[layer] = (
            d_projected[:, :query_width],
            d_projected[:, query_width : query_width + kv_width],
            d_projected[:, query_width + kv_width :],
            d_out,
            d_gate,
            d_up,
            d_down,
        )
        gain_grads[layer] = (d_attn_gain, d_mlp_gain, d_query_gain, d_key_gain)

    with jax.named_scope("gain_grads"):
        wide = jnp.stack([g[0] for g in gain_grads] + [g[1] for g in gain_grads])
        wide = wide.reshape(2 * layers, contexts, shard).transpose(1, 0, 2)
        narrow = jnp.stack([g[2] for g in gain_grads] + [g[3] for g in gain_grads])
        wide = wide.reshape(contexts, 1, 2 * layers * shard)
        narrow = jnp.broadcast_to(
            narrow.reshape(1, 1, 2 * layers * head_dim), (contexts, 1, 2 * layers * head_dim)
        )
        pieces = jnp.concatenate([wide, narrow], axis=2)
        pieces = jnp.broadcast_to(pieces, (contexts, tensors, pieces.shape[2]))
        pieces = pieces.reshape(contexts * tensors, -1)
        sums = jnp.sum(lax.all_to_all(pieces, AXES, 0, 0, tiled=True), axis=0)
        wide = sums[: 2 * layers * shard].reshape(2, layers, shard)
        narrow = sums[2 * layers * shard :].reshape(2, layers, head_dim)
    stacked = [jnp.stack([grads[member] for grads in weight_grads]) for member in range(7)]
    return (current, grad_res, *stacked, wide[0], wide[1], narrow[0], narrow[1])


def solution(mesh):
    rows = P(("context", "tensor"), None)
    in_split = P(None, "context", "tensor")
    out_split = P(None, "tensor", "context")
    gain = P(None, "context")
    return jax.shard_map(
        body,
        mesh=mesh,
        in_specs=(
            rows,
            rows,
            P(),
            in_split,
            in_split,
            in_split,
            out_split,
            in_split,
            in_split,
            out_split,
            gain,
            gain,
            P(),
            P(),
        ),
        out_specs=(
            rows,
            rows,
            in_split,
            in_split,
            in_split,
            out_split,
            in_split,
            in_split,
            out_split,
            gain,
            gain,
            P(),
            P(),
        ),
        check_vma=False,
    )
```

```python
import functools

import jax
import jax.numpy as jnp
from jax import lax
from jax.experimental import pallas as pl
from jax.experimental.pallas import tpu as pltpu
from jax.sharding import PartitionSpec as P

EPSILON = 1e-06
THETA = 1000000.0
AXES = ("context", "tensor")
BF = jnp.bfloat16
F32 = jnp.float32


def mm(a, b):
    return jnp.dot(a, b, preferred_element_type=F32)


def mm_tn(a, b):
    return lax.dot_general(a, b, (((0,), (0,)), ((), ())), preferred_element_type=F32)


def mm_nt(a, b):
    return lax.dot_general(a, b, (((1,), (1,)), ((), ())), preferred_element_type=F32)


def rms_scale(row_data, gain_row):
    mean_square = jnp.mean(row_data * row_data, axis=-1, keepdims=True)
    return row_data * lax.rsqrt(mean_square + EPSILON) * gain_row


def rotary_tables(positions, head_dim):
    half_dim = head_dim // 2
    exponent = jnp.arange(half_dim, dtype=F32) * (2.0 / head_dim)
    inverse = jnp.power(F32(THETA), -exponent)
    angles = positions.astype(F32)[:, None] * inverse[None, :]
    return (jnp.cos(angles), jnp.sin(angles))


def row_positions(block_order, first_row, row_count, rows_per_block):
    rows_index = first_row + jnp.arange(row_count, dtype=jnp.int32)
    slot_index = rows_index // rows_per_block
    slots = jnp.arange(block_order.shape[0], dtype=jnp.int32)
    matches = slot_index[:, None] == slots[None, :]
    owners = jnp.sum(jnp.where(matches, block_order[None, :], 0), axis=1)
    return owners * rows_per_block + rows_index % rows_per_block


def after(value, *others):
    return lax.optimization_barrier((value, others))[0]


def rows_call(kernel, out_shapes, *operands):
    return pl.pallas_call(
        kernel,
        out_shape=[jax.ShapeDtypeStruct(shape, kind) for shape, kind in out_shapes],
        compiler_params=pltpu.CompilerParams(vmem_limit_bytes=48 * 1024 * 1024),
    )(*operands)


def join_kernel(*refs):
    *pieces, out_ref = refs
    count = pieces[0].shape[0]
    for slot, piece in enumerate(pieces):
        out_ref[slot * count : (slot + 1) * count, :] = piece[...]


def join(pieces):
    rows, width = pieces[0].shape
    return rows_call(join_kernel, [((len(pieces) * rows, width), pieces[0].dtype)], *pieces)[0]


def prep_kernel(heads, x_ref, gain_ref, cos_ref, sin_ref, out_ref):
    head_dim = gain_ref.shape[1]
    for head in range(x_ref.shape[1] // head_dim):
        at = slice(head * head_dim, (head + 1) * head_dim)
        rows = x_ref[:, at]
        if head < heads:
            mean_square = jnp.mean(rows * rows, axis=-1, keepdims=True)
            rows = rows * lax.rsqrt(mean_square + EPSILON) * gain_ref[...]
            rows = rows * cos_ref[...] + pltpu.roll(rows, head_dim // 2, 1) * sin_ref[...]
        out_ref[:, at] = rows.astype(BF)


def prep_heads(projected, heads, gain, tables):
    kernel = functools.partial(prep_kernel, heads)
    return rows_call(kernel, [(projected.shape, BF)], projected, gain, *tables)[0]


def prep_back_kernel(heads, x_ref, gain_ref, cos_ref, sin_ref, *refs):
    grads, (out_ref, gain_grad_ref) = refs[:-2], refs[-2:]
    head_dim = gain_ref.shape[1]
    gain_grad = jnp.zeros((1, head_dim), F32)
    for head in range(x_ref.shape[1] // head_dim):
        at = slice(head * head_dim, (head + 1) * head_dim)
        grad = grads[0][:, at].astype(F32)
        for piece in grads[1:]:
            grad = grad + piece[:, at].astype(F32)
        if head < heads:
            rows = x_ref[:, at]
            mean_square = jnp.mean(rows * rows, axis=-1, keepdims=True)
            scale = lax.rsqrt(mean_square + EPSILON)
            unit = rows * scale
            grad = grad * cos_ref[...] + pltpu.roll(grad * sin_ref[...], head_dim // 2, 1)
            gain_grad = gain_grad + jnp.sum(grad * unit, axis=0, keepdims=True)
            grad = grad * gain_ref[...]
            grad = scale * (grad - unit * jnp.mean(grad * unit, axis=-1, keepdims=True))
        out_ref[:, at] = grad.astype(BF)
    gain_grad_ref[...] = gain_grad


def prep_heads_back(projected, heads, gain, tables, grads):
    kernel = functools.partial(prep_back_kernel, heads)
    shapes = [(projected.shape, BF), (gain.shape, F32)]
    return rows_call(kernel, shapes, projected, gain, *tables, *grads)


def dot_nt(a, b):
    return lax.dot_general(a, b, (((1,), (1,)), ((), ())), preferred_element_type=F32)


def dot_tn(a, b):
    return lax.dot_general(a, b, (((0,), (0,)), ((), ())), preferred_element_type=F32)


def stack_heads(ref, first, groups, head_dim):
    return jnp.concatenate(
        [ref[:, (first + i) * head_dim : (first + i + 1) * head_dim] for i in range(groups)], axis=0
    )


def attend_kernel(head_dim, query_ref, query_pos_ref, key_pos_ref, *refs):
    pairs, (out_ref, log_ref) = refs[:-2], refs[-2:]
    count = query_ref.shape[0]
    kv_heads = pairs[0].shape[1] // (2 * head_dim)
    groups = query_ref.shape[1] // (kv_heads * head_dim)
    query_pos = jnp.concatenate([query_pos_ref[...]] * groups, axis=0)
    for kv_head in range(kv_heads):
        queries = stack_heads(query_ref, kv_head * groups, groups, head_dim)
        totals = jnp.zeros((groups * count, 1), F32)
        summed = jnp.zeros((groups * count, head_dim), F32)
        for slot, pair in enumerate(pairs):
            keys = pair[:, kv_head * head_dim : (kv_head + 1) * head_dim]
            values = pair[:, (kv_heads + kv_head) * head_dim : (kv_heads + kv_head + 1) * head_dim]
            scores = dot_nt(queries, keys) * head_dim ** (-0.5)
            causal = key_pos_ref[slot : slot + 1, :] <= query_pos
            weights = jnp.where(causal, jnp.exp(scores), 0.0)
            totals = totals + jnp.sum(weights, axis=-1, keepdims=True)
            summed = summed + jnp.dot(weights.astype(BF), values, preferred_element_type=F32)
        outputs = summed / totals
        logs = jnp.log(totals)
        for group in range(groups):
            head = kv_head * groups + group
            at = slice(group * count, (group + 1) * count)
            out_ref[:, head * head_dim : (head + 1) * head_dim] = outputs[at].astype(BF)
            log_ref[:, head : head + 1] = logs[at]


def attend(queries, pairs, query_pos, key_pos, head_dim):
    heads = queries.shape[1] // head_dim
    shapes = [(queries.shape, BF), ((queries.shape[0], heads), F32)]
    kernel = functools.partial(attend_kernel, head_dim)
    return rows_call(kernel, shapes, queries, query_pos, key_pos, *pairs)


def attend_back_kernel(
    head_dim, query_ref, query_pos_ref, key_pos_ref, out_ref, log_ref, grad_ref, *refs
):
    slots = (len(refs) - 1) // 2
    pairs, query_grad_ref, pair_grads = refs[:slots], refs[slots], refs[slots + 1 :]
    count = query_ref.shape[0]
    scale = head_dim ** (-0.5)
    kv_heads = pairs[0].shape[1] // (2 * head_dim)
    groups = query_ref.shape[1] // (kv_heads * head_dim)
    query_pos = jnp.concatenate([query_pos_ref[...]] * groups, axis=0)
    for kv_head in range(kv_heads):
        first = kv_head * groups
        queries = stack_heads(query_ref, first, groups, head_dim)
        grads = stack_heads(grad_ref, first, groups, head_dim)
        outputs = stack_heads(out_ref, first, groups, head_dim)
        logs = jnp.concatenate(
            [log_ref[:, first + i : first + i + 1] for i in range(groups)], axis=0
        )
        deltas = jnp.sum(grads.astype(F32) * outputs.astype(F32), axis=-1, keepdims=True)
        query_grad = jnp.zeros((groups * count, head_dim), F32)
        key_at = slice(kv_head * head_dim, (kv_head + 1) * head_dim)
        value_at = slice((kv_heads + kv_head) * head_dim, (kv_heads + kv_head + 1) * head_dim)
        for slot in range(slots):
            keys, values = pairs[slot][:, key_at], pairs[slot][:, value_at]
            scores = dot_nt(queries, keys) * scale
            causal = key_pos_ref[slot : slot + 1, :] <= query_pos
            probs = jnp.where(causal, jnp.exp(scores - logs), 0.0)
            value_grad = dot_tn(probs.astype(BF), grads)
            grad_probs = dot_nt(grads, values)
            grad_scores = (probs * (grad_probs - deltas) * scale).astype(BF)
            query_grad = query_grad + jnp.dot(grad_scores, keys, preferred_element_type=F32)
            key_grad = dot_tn(grad_scores, queries)
            pair_grads[slot][:, key_at] = key_grad.astype(pair_grads[slot].dtype)
            pair_grads[slot][:, value_at] = value_grad.astype(pair_grads[slot].dtype)
        for group in range(groups):
            head = first + group
            query_grad_ref[:, head * head_dim : (head + 1) * head_dim] = query_grad[
                group * count : (group + 1) * count
            ]


def attend_back(queries, pairs, query_pos, key_pos, outputs, logs, grads, head_dim):
    kernel = functools.partial(attend_back_kernel, head_dim)
    shapes = [(queries.shape, F32)]
    shapes += [(pair.shape, BF if slot else F32) for slot, pair in enumerate(pairs)]
    query_grad, *pair_grads = rows_call(
        kernel, shapes, queries, query_pos, key_pos, outputs, logs, grads, *pairs
    )
    return query_grad, pair_grads


class Links:
    def __init__(self, contexts, tensors):
        self.contexts, self.tensors = contexts, tensors
        self.count = contexts * tensors
        self.near = 4
        self.rows = tensors // 2
        self.half = contexts // 2
        self.far_half = self.half * tensors
        self.half_groups = [
            [(part * self.half + member) * tensors + tensor for member in range(self.half)]
            for part in range(2)
            for tensor in range(tensors)
        ]
        self.context = lax.axis_index("context")
        self.upper = self.context >= self.half

    def swap(self, value, mask):
        return lax.ppermute(value, AXES, [(i, i ^ mask) for i in range(self.count)])

    def far_masks(self):
        return [far * self.near * self.tensors for far in range(self.contexts // self.near)]

    def half_masks(self):
        return [member * self.tensors for member in range(self.half)]

    def by_part(self, mine, theirs):
        return jnp.where(self.upper, theirs, mine), jnp.where(self.upper, mine, theirs)

    def spread(self, value, masks):
        return [value] + [self.swap(value, mask) for mask in masks[1:]]

    def cube_masks(self):
        return [
            near * self.tensors + row * 2
            for near in range(self.near)
            for row in range(self.rows)
        ]

    def collect(self, chunks, masks):
        total = chunks[0].astype(F32)
        for chunk, mask in zip(chunks[1:], masks[1:]):
            total = total + self.swap(chunk.astype(BF), mask).astype(F32)
        return total

    def exchange_context(self, chunks):
        return lax.all_to_all(chunks, "context", 0, 0)

    def spread_context(self, value):
        return self.exchange_context(
            jnp.broadcast_to(value[None], (self.contexts, *value.shape))
        )

    def relative(self, slots, index):
        count, shape = slots.shape[0], slots.shape[1:]
        bit = 1
        while bit < count:
            pairs = slots.reshape(count // (2 * bit), 2, bit, *shape)
            flipped = jnp.concatenate([pairs[:, 1:], pairs[:, :1]], axis=1)
            odd = (index // bit) % 2 == 1
            slots = jnp.where(odd, flipped, pairs).reshape(count, *shape)
            bit *= 2
        return slots

    def gather_rows(self, rows):
        line = join(self.spread(rows, self.far_masks()))
        own = join(self.spread(line, self.cube_masks()))
        return own, self.swap(own, 1)

    def reduce_rows(self, own, other):
        half = own + self.swap(other.astype(BF), 1).astype(F32)
        masks = self.cube_masks()
        line = self.collect(jnp.split(half, len(masks), axis=0), masks)
        masks = self.far_masks()
        return self.collect(jnp.split(line, len(masks), axis=0), masks)

    def spread_rows(self, rows):
        for mask in (self.far_half, 2, 1):
            rows = join([rows, self.swap(rows, mask)])
        return rows

    def return_rows(self, partial):
        for mask in (1, 2, self.far_half):
            own, other = jnp.split(partial, 2, axis=0)
            partial = own + self.swap(other.astype(BF), mask).astype(F32)
        return partial

    def gather_half(self, mine, theirs):
        got = self.swap(theirs, self.far_half)
        low, high = self.by_part(mine, got)
        return jnp.stack([low, high])

    def scatter_half(self, partial):
        rows, columns = partial.shape
        shard = lax.psum_scatter(
            partial.astype(BF).reshape(2, rows // 2, columns),
            AXES,
            scatter_dimension=1,
            axis_index_groups=self.half_groups,
            tiled=True,
        )
        mine = jnp.where(self.upper, shard[1], shard[0])
        theirs = jnp.where(self.upper, shard[0], shard[1])
        got = self.swap(theirs, self.far_half)
        return [part.astype(F32) for part in self.by_part(mine, got)]


def body(
    residual_in,
    grad_output,
    block_order,
    w_query,
    key_weight,
    value_weight,
    w_out,
    w_gate,
    w_up,
    w_down,
    attn_gain,
    mlp_gain,
    query_gain,
    key_gain,
):
    contexts, tensors = lax.axis_size("context"), lax.axis_size("tensor")
    links = Links(contexts, tensors)
    masks = links.half_masks()
    layers = w_query.shape[0]
    head_dim = query_gain.shape[1]
    local_rows, width = residual_in.shape
    context_rows = local_rows * tensors
    rows_per_block = context_rows // 2
    all_rows = context_rows * contexts
    key_pos = row_positions(block_order, jnp.int32(0), all_rows, rows_per_block)
    key_pos = links.relative(key_pos.reshape(contexts, context_rows), links.context)
    key_pos = key_pos.reshape(contexts, tensors, local_rows)
    tensor = lax.axis_index("tensor")
    key_pos = links.relative(key_pos.transpose(1, 0, 2), tensor)
    key_pos = key_pos.reshape(2, 2, 2, links.half, local_rows).transpose(3, 1, 0, 2, 4)
    key_pos = key_pos.reshape(links.half, 2 * context_rows)
    query_pos = key_pos[0]
    cosine, sine = rotary_tables(query_pos, head_dim)
    tables = (
        jnp.concatenate([cosine, cosine], axis=1),
        jnp.concatenate([-sine, sine], axis=1),
    )
    query_pos = query_pos[:, None]
    query_width, kv_width = w_query.shape[2] // 2, key_weight.shape[2] // 2
    query_heads = query_width // head_dim
    kv_heads = kv_width // head_dim
    units = w_gate.shape[2] // contexts
    shard = w_query.shape[1]
    query_gains = [query_gain[layer][None] for layer in range(layers)]
    key_gains = [key_gain[layer][None] for layer in range(layers)]

    gains = jnp.concatenate([attn_gain, mlp_gain], axis=0)
    gains = links.spread_context(gains).transpose(1, 0, 2).reshape(2 * layers, width)
    gains = gains.astype(F32)

    def ffn_parts(layer):
        parts = [w_gate[layer], w_up[layer], w_down[layer].T]
        parts = [part.reshape(shard, contexts, units) for part in parts]
        return jnp.concatenate(parts, axis=2).transpose(1, 0, 2)

    attn_weights, out_weights, ffn_weights = [], [], []
    for layer in range(layers):
        parts = []
        for part in range(2):
            query_at = slice(part * query_width, (part + 1) * query_width)
            kv_at = slice(part * kv_width, (part + 1) * kv_width)
            columns = [
                w_query[layer][:, query_at],
                key_weight[layer][:, kv_at],
                value_weight[layer][:, kv_at],
                w_out[layer].T[:, query_at],
            ]
            parts.append(jnp.concatenate(columns, axis=1))
        mine, theirs = links.by_part(*parts)
        shards = links.gather_half(mine, theirs)
        gathered = []
        for columns in (
            shards[:, :, : query_width + 2 * kv_width], shards[:, :, query_width + 2 * kv_width :]
        ):
            gathered.append(
                lax.all_gather(
                    columns,
                    AXES,
                    axis=1,
                    tiled=True,
                    axis_index_groups=links.half_groups,
                )
            )
        if layer == 0:
            gathered_0 = gathered[0]
        attn_weights.append(gathered[0].reshape(width, -1))
        out_weights.append(gathered[1].reshape(width, -1))

    current = residual_in
    stored = []
    for layer in range(layers):
        gain_attn, gain_mlp = gains[layer], gains[layers + layer]
        normed_in = links.spread_rows(rms_scale(current, gain_attn).astype(BF))
        parts = ffn_parts(layer)
        parts = after(parts, gathered_0 if layer == 0 else stored[0][9][0])
        ffn_weights.append(links.exchange_context(parts).reshape(width, 3 * units))
        projected = mm(normed_in, attn_weights[layer])
        pair_proj, query_proj = projected[:, query_width:], projected[:, :query_width]
        pairs = prep_heads(pair_proj, kv_heads, key_gains[layer], tables)
        pairs = links.spread(pairs, masks)
        queries = prep_heads(query_proj, query_heads, query_gains[layer], tables)
        if layer + 1 == layers:
            top_gradient = links.gather_rows(after(grad_output, query_proj).astype(BF))
            queries = after(queries, top_gradient[0])
        output_rows, log_totals = attend(queries, pairs, query_pos, key_pos, head_dim)
        partial = mm_nt(output_rows, out_weights[layer])
        middle = current + links.return_rows(partial)
        normed_mid = links.gather_rows(rms_scale(middle, gain_mlp).astype(BF))
        inner, partial = [], []
        weights = ffn_weights[layer]
        for rows in normed_mid:
            both = mm(rows, weights[:, : 2 * units])
            gate, up = both[:, :units], both[:, units:]
            hidden = (jax.nn.silu(gate) * up).astype(BF)
            inner.append((gate, up, hidden))
            partial.append(mm_nt(hidden, weights[:, 2 * units :]))
        if layer + 1 < layers:
            block_out = middle + links.reduce_rows(*partial)
        else:
            last = (middle, partial)
        stored.append(
            (
                current,
                normed_in,
                query_proj,
                pair_proj,
                queries,
                pairs,
                output_rows,
                log_totals,
                middle,
                normed_mid,
                inner,
            )
        )
        if layer + 1 < layers:
            current = block_out

    grad_res = grad_output
    weight_grads, gain_grads = [None] * layers, [None] * layers
    for layer in reversed(range(layers)):
        (
            layer_in,
            normed_in,
            query_proj,
            pair_proj,
            queries,
            pairs,
            output_rows,
            log_totals,
            middle,
            normed_mid,
            inner,
        ) = stored[layer]
        gain_attn, gain_mlp = gains[layer], gains[layers + layer]
        if layer + 1 == layers:
            grad_all = top_gradient
        else:
            grad_all = links.gather_rows(grad_res.astype(BF))
        partial, d_in, d_down = [], 0.0, 0.0
        weights = ffn_weights[layer]
        for rows, grad_rows, (gate, up, hidden) in zip(normed_mid, grad_all, inner):
            grad_hidden = mm(grad_rows, weights[:, 2 * units :])
            sigmoid = jax.nn.sigmoid(gate)
            grad_up = (grad_hidden * gate * sigmoid).astype(BF)
            grad_gate = (
                grad_hidden * up * sigmoid * (1.0 + gate * (1.0 - sigmoid))
            ).astype(BF)
            both = jnp.concatenate([grad_gate, grad_up], axis=1)
            partial.append(mm_nt(both, weights[:, : 2 * units]))
            d_in = d_in + mm_tn(rows, both)
            d_down = d_down + mm_tn(grad_rows, hidden)
        grad_normed_mid = links.reduce_rows(*partial)
        unused, norm_back = jax.vjp(rms_scale, middle, gain_mlp)
        grad_mid_part, d_mlp_gain = norm_back(grad_normed_mid)
        grad_mid = grad_res + grad_mid_part
        pieces = jnp.concatenate([d_in, d_down], axis=1).astype(BF)
        if layer + 1 < layers:
            pieces = after(pieces, moved)
        pieces = links.exchange_context(pieces.reshape(contexts, shard, 3 * units))
        moved = pieces
        pieces = pieces.transpose(1, 0, 2)
        d_gate = pieces[:, :, :units].reshape(shard, contexts * units).astype(F32)
        d_up = pieces[:, :, units : 2 * units].reshape(shard, contexts * units).astype(F32)
        d_down = pieces[:, :, 2 * units :].reshape(shard, contexts * units).T.astype(F32)
        if layer + 1 == layers:
            middle_last, partial_last = last
            partial_last = after(partial_last, grad_mid)
            final_out = middle_last + links.reduce_rows(*partial_last)
        grad_mid_all = links.spread_rows(grad_mid.astype(BF))
        d_out = links.scatter_half(mm_tn(grad_mid_all, output_rows))
        d_out = jnp.concatenate(d_out, axis=1).T
        attention_gradient = mm(grad_mid_all, out_weights[layer]).astype(BF)
        query_grad, pair_grads = attend_back(
            queries,
            pairs,
            query_pos,
            key_pos,
            output_rows,
            log_totals,
            attention_gradient,
            head_dim,
        )
        pair_grads = [pair_grads[0]] + [
            links.swap(grad, mask) for grad, mask in zip(pair_grads[1:], masks[1:])
        ]
        grad_queries, d_query_gain = prep_heads_back(
            query_proj, query_heads, query_gains[layer], tables, [query_grad]
        )
        grad_pairs, d_key_gain = prep_heads_back(
            pair_proj, kv_heads, key_gains[layer], tables, pair_grads
        )
        grad_projected = jnp.concatenate([grad_queries, grad_pairs], axis=1)
        partial = mm_nt(grad_projected, attn_weights[layer])
        if layer + 1 == layers:
            partial = after(partial, final_out)
        grad_normed_in = links.return_rows(partial)
        unused, input_back = jax.vjp(rms_scale, layer_in, gain_attn)
        grad_in_part, d_attn_gain = input_back(grad_normed_in)
        grad_res = grad_mid + grad_in_part
        halves = links.scatter_half(mm_tn(normed_in, grad_projected))
        cuts = [query_width, query_width + kv_width]
        d_query, d_key, d_value = [
            jnp.concatenate(pair, axis=1)
            for pair in zip(*[jnp.split(half, cuts, axis=1) for half in halves])
        ]
        weight_grads[layer] = (
            d_query,
            d_key,
            d_value,
            d_out,
            d_gate,
            d_up,
            d_down,
        )
        gain_grads[layer] = (d_attn_gain, d_mlp_gain, d_query_gain[0], d_key_gain[0])

    wide = jnp.stack([g[0] for g in gain_grads] + [g[1] for g in gain_grads])
    wide = wide.reshape(2 * layers, contexts, shard).transpose(1, 0, 2)
    narrow = jnp.stack([g[2] for g in gain_grads] + [g[3] for g in gain_grads])
    wide = wide.reshape(contexts, 1, 2 * layers * shard)
    narrow = jnp.broadcast_to(
        narrow.reshape(1, 1, 2 * layers * head_dim), (contexts, 1, 2 * layers * head_dim)
    )
    pieces = jnp.concatenate([wide, narrow], axis=2)
    pieces = jnp.broadcast_to(pieces, (contexts, tensors, pieces.shape[2]))
    pieces = after(pieces.reshape(contexts * tensors, -1), moved)
    sums = jnp.sum(lax.all_to_all(pieces, AXES, 0, 0, tiled=True), axis=0)
    wide = sums[: 2 * layers * shard].reshape(2, layers, shard)
    narrow = sums[2 * layers * shard :].reshape(2, layers, head_dim)
    stacked = [jnp.stack([grads[member] for grads in weight_grads]) for member in range(7)]
    return (final_out, grad_res, *stacked, wide[0], wide[1], narrow[0], narrow[1])


def solution(mesh):
    rows = P(("context", "tensor"), None)
    in_split = P(None, "context", "tensor")
    out_split = P(None, "tensor", "context")
    gain = P(None, "context")
    weights = (in_split, in_split, in_split, out_split, in_split, in_split, out_split)
    return jax.shard_map(
        body,
        mesh=mesh,
        in_specs=(rows, rows, P(), *weights, gain, gain, P(), P()),
        out_specs=(rows, rows, *weights, gain, gain, P(), P()),
        check_vma=False,
    )
```

```python
import functools

import jax
import jax.numpy as jnp
from jax import lax
from jax.experimental import pallas as pl
from jax.experimental.pallas import tpu as pltpu
from jax.sharding import PartitionSpec as P

EPSILON = 1e-06
THETA = 1000000.0
CONTEXT, TENSOR = AXES = ("context", "tensor")
BF = jnp.bfloat16
F32 = jnp.float32


def mm(a, b):
    return jnp.dot(a, b, preferred_element_type=F32)


def mm_tn(a, b):
    return lax.dot_general(a, b, (((0,), (0,)), ((), ())), preferred_element_type=F32)


def mm_nt(a, b):
    return lax.dot_general(a, b, (((1,), (1,)), ((), ())), preferred_element_type=F32)


def rms_scale(row_data, gain_row):
    mean_square = jnp.mean(row_data * row_data, axis=-1, keepdims=True)
    return row_data * lax.rsqrt(mean_square + EPSILON) * gain_row


def rotary_tables(positions, head_dim):
    half_dim = head_dim // 2
    exponent = jnp.arange(half_dim, dtype=F32) * (2.0 / head_dim)
    inverse = jnp.power(F32(THETA), -exponent)
    angles = positions.astype(F32)[:, None] * inverse[None, :]
    return (jnp.cos(angles), jnp.sin(angles))


def row_positions(block_order, first_row, row_count, rows_per_block):
    rows_index = first_row + jnp.arange(row_count, dtype=jnp.int32)
    slot_index = rows_index // rows_per_block
    slots = jnp.arange(block_order.shape[0], dtype=jnp.int32)
    matches = slot_index[:, None] == slots[None, :]
    owners = jnp.sum(jnp.where(matches, block_order[None, :], 0), axis=1)
    return owners * rows_per_block + rows_index % rows_per_block


def after(value, *others):
    return lax.optimization_barrier((value, others))[0]


def rows_call(kernel, out_shapes, *operands):
    return pl.pallas_call(
        kernel,
        out_shape=[jax.ShapeDtypeStruct(shape, kind) for shape, kind in out_shapes],
        compiler_params=pltpu.CompilerParams(vmem_limit_bytes=48 * 1024 * 1024),
    )(*operands)


def join_kernel(*refs):
    *pieces, out_ref = refs
    count = pieces[0].shape[0]
    for slot, piece in enumerate(pieces):
        out_ref[slot * count : (slot + 1) * count, :] = piece[...]


def join(pieces):
    rows, width = pieces[0].shape
    return rows_call(join_kernel, [((len(pieces) * rows, width), pieces[0].dtype)], *pieces)[0]


def index_call(kernel, out_shapes, index, *operands):
    vmem = pl.BlockSpec(memory_space=pltpu.VMEM)
    return pl.pallas_call(
        kernel,
        in_specs=[pl.BlockSpec(memory_space=pltpu.SMEM)] + [vmem] * len(operands),
        out_specs=[vmem] * len(out_shapes),
        out_shape=[jax.ShapeDtypeStruct(shape, kind) for shape, kind in out_shapes],
        compiler_params=pltpu.CompilerParams(vmem_limit_bytes=48 * 1024 * 1024),
    )(index.reshape(1), *operands)


def join_at_kernel(index_ref, *refs):
    *pieces, out_ref = refs
    count = pieces[0].shape[1]
    for slot, piece in enumerate(pieces):
        first = pl.multiple_of((index_ref[0] ^ slot) * count, count)
        out_ref[:, pl.ds(first, count), :] = piece[...]


def join_at(pieces, index):
    parts, rows, width = pieces[0].shape
    shape = (parts, len(pieces) * rows, width)
    return index_call(join_at_kernel, [(shape, pieces[0].dtype)], index, *pieces)[0]


def split_at_kernel(index_ref, x_ref, *outs):
    count = outs[0].shape[1]
    for slot, out in enumerate(outs):
        first = pl.multiple_of((index_ref[0] ^ slot) * count, count)
        out[...] = x_ref[:, pl.ds(first, count), :].astype(out.dtype)


def split_at(x, places, index, own=F32):
    parts, rows, width = x.shape
    shape = (parts, rows // places, width)
    shapes = [(shape, BF if slot else own) for slot in range(places)]
    return index_call(split_at_kernel, shapes, index, x)


def prep_kernel(heads, x_ref, gain_ref, cos_ref, sin_ref, out_ref):
    head_dim = gain_ref.shape[1]
    for head in range(x_ref.shape[1] // head_dim):
        at = slice(head * head_dim, (head + 1) * head_dim)
        rows = x_ref[:, at]
        if head < heads:
            mean_square = jnp.mean(rows * rows, axis=-1, keepdims=True)
            rows = rows * lax.rsqrt(mean_square + EPSILON) * gain_ref[...]
            rows = rows * cos_ref[...] + pltpu.roll(rows, head_dim // 2, 1) * sin_ref[...]
        out_ref[:, at] = rows.astype(BF)


def prep_heads(projected, heads, gain, tables):
    kernel = functools.partial(prep_kernel, heads)
    return rows_call(kernel, [(projected.shape, BF)], projected, gain, *tables)[0]


def prep_back_kernel(heads, x_ref, gain_ref, cos_ref, sin_ref, *refs):
    grads, (out_ref, gain_grad_ref) = refs[:-2], refs[-2:]
    head_dim = gain_ref.shape[1]
    gain_grad = jnp.zeros((1, head_dim), F32)
    for head in range(x_ref.shape[1] // head_dim):
        at = slice(head * head_dim, (head + 1) * head_dim)
        grad = grads[0][:, at].astype(F32)
        for piece in grads[1:]:
            grad = grad + piece[:, at].astype(F32)
        if head < heads:
            rows = x_ref[:, at]
            mean_square = jnp.mean(rows * rows, axis=-1, keepdims=True)
            scale = lax.rsqrt(mean_square + EPSILON)
            unit = rows * scale
            grad = grad * cos_ref[...] + pltpu.roll(grad * sin_ref[...], head_dim // 2, 1)
            gain_grad = gain_grad + jnp.sum(grad * unit, axis=0, keepdims=True)
            grad = grad * gain_ref[...]
            grad = scale * (grad - unit * jnp.mean(grad * unit, axis=-1, keepdims=True))
        out_ref[:, at] = grad.astype(BF)
    gain_grad_ref[...] = gain_grad


def prep_heads_back(projected, heads, gain, tables, grads):
    kernel = functools.partial(prep_back_kernel, heads)
    shapes = [(projected.shape, BF), (gain.shape, F32)]
    return rows_call(kernel, shapes, projected, gain, *tables, *grads)


def dot_nt(a, b):
    return lax.dot_general(a, b, (((1,), (1,)), ((), ())), preferred_element_type=F32)


def dot_tn(a, b):
    return lax.dot_general(a, b, (((0,), (0,)), ((), ())), preferred_element_type=F32)


def stack_heads(ref, first, groups, head_dim):
    return jnp.concatenate(
        [ref[:, (first + i) * head_dim : (first + i + 1) * head_dim] for i in range(groups)], axis=0
    )


def attend_kernel(head_dim, query_ref, query_pos_ref, key_pos_ref, *refs):
    pairs, (out_ref, log_ref) = refs[:-2], refs[-2:]
    count = query_ref.shape[0]
    kv_heads = pairs[0].shape[1] // (2 * head_dim)
    groups = query_ref.shape[1] // (kv_heads * head_dim)
    query_pos = jnp.concatenate([query_pos_ref[...]] * groups, axis=0)
    for kv_head in range(kv_heads):
        queries = stack_heads(query_ref, kv_head * groups, groups, head_dim)
        totals = jnp.zeros((groups * count, 1), F32)
        summed = jnp.zeros((groups * count, head_dim), F32)
        for slot, pair in enumerate(pairs):
            keys = pair[:, kv_head * head_dim : (kv_head + 1) * head_dim]
            values = pair[:, (kv_heads + kv_head) * head_dim : (kv_heads + kv_head + 1) * head_dim]
            scores = dot_nt(queries, keys) * head_dim ** (-0.5)
            causal = key_pos_ref[slot : slot + 1, :] <= query_pos
            weights = jnp.where(causal, jnp.exp(scores), 0.0)
            totals = totals + jnp.sum(weights, axis=-1, keepdims=True)
            summed = summed + jnp.dot(weights.astype(BF), values, preferred_element_type=F32)
        outputs = summed / totals
        logs = jnp.log(totals)
        for group in range(groups):
            head = kv_head * groups + group
            at = slice(group * count, (group + 1) * count)
            out_ref[:, head * head_dim : (head + 1) * head_dim] = outputs[at].astype(BF)
            log_ref[:, head : head + 1] = logs[at]


def attend(queries, pairs, query_pos, key_pos, head_dim):
    heads = queries.shape[1] // head_dim
    shapes = [(queries.shape, BF), ((queries.shape[0], heads), F32)]
    kernel = functools.partial(attend_kernel, head_dim)
    return rows_call(kernel, shapes, queries, query_pos, key_pos, *pairs)


def attend_back_kernel(
    head_dim, query_ref, query_pos_ref, key_pos_ref, out_ref, log_ref, grad_ref, *refs
):
    slots = (len(refs) - 1) // 2
    pairs, query_grad_ref, pair_grads = refs[:slots], refs[slots], refs[slots + 1 :]
    count = query_ref.shape[0]
    scale = head_dim ** (-0.5)
    kv_heads = pairs[0].shape[1] // (2 * head_dim)
    groups = query_ref.shape[1] // (kv_heads * head_dim)
    query_pos = jnp.concatenate([query_pos_ref[...]] * groups, axis=0)
    for kv_head in range(kv_heads):
        first = kv_head * groups
        queries = stack_heads(query_ref, first, groups, head_dim)
        grads = stack_heads(grad_ref, first, groups, head_dim)
        outputs = stack_heads(out_ref, first, groups, head_dim)
        logs = jnp.concatenate(
            [log_ref[:, first + i : first + i + 1] for i in range(groups)], axis=0
        )
        deltas = jnp.sum(grads.astype(F32) * outputs.astype(F32), axis=-1, keepdims=True)
        query_grad = jnp.zeros((groups * count, head_dim), F32)
        key_at = slice(kv_head * head_dim, (kv_head + 1) * head_dim)
        value_at = slice((kv_heads + kv_head) * head_dim, (kv_heads + kv_head + 1) * head_dim)
        for slot in range(slots):
            keys, values = pairs[slot][:, key_at], pairs[slot][:, value_at]
            scores = dot_nt(queries, keys) * scale
            causal = key_pos_ref[slot : slot + 1, :] <= query_pos
            probs = jnp.where(causal, jnp.exp(scores - logs), 0.0)
            value_grad = dot_tn(probs.astype(BF), grads)
            grad_probs = dot_nt(grads, values)
            grad_scores = (probs * (grad_probs - deltas) * scale).astype(BF)
            query_grad = query_grad + jnp.dot(grad_scores, keys, preferred_element_type=F32)
            key_grad = dot_tn(grad_scores, queries)
            pair_grads[slot][:, key_at] = key_grad.astype(pair_grads[slot].dtype)
            pair_grads[slot][:, value_at] = value_grad.astype(pair_grads[slot].dtype)
        for group in range(groups):
            head = first + group
            query_grad_ref[:, head * head_dim : (head + 1) * head_dim] = query_grad[
                group * count : (group + 1) * count
            ]


def attend_back(queries, pairs, query_pos, key_pos, outputs, logs, grads, head_dim):
    kernel = functools.partial(attend_back_kernel, head_dim)
    shapes = [(queries.shape, F32)]
    shapes += [(pair.shape, BF if slot else F32) for slot, pair in enumerate(pairs)]
    query_grad, *pair_grads = rows_call(
        kernel, shapes, queries, query_pos, key_pos, outputs, logs, grads, *pairs
    )
    return query_grad, pair_grads


class Links:
    def __init__(self, contexts, tensors):
        self.contexts, self.tensors = contexts, tensors
        self.count = contexts * tensors
        self.half = contexts // 2
        self.far_half = self.half * tensors
        self.half_groups = [
            [(part * self.half + member) * tensors + tensor for member in range(self.half)]
            for part in range(2)
            for tensor in range(tensors)
        ]
        self.context = lax.axis_index(CONTEXT)
        self.upper = self.context >= self.half
        self.place = self.context % self.half

    def swap(self, value, mask):
        return lax.ppermute(value, AXES, [(i, i ^ mask) for i in range(self.count)])

    def line_masks(self):
        return [2 * place * self.tensors for place in range(self.half)]

    def square_masks(self):
        return [
            side * self.tensors + row * 2 for side in range(2) for row in range(self.tensors // 2)
        ]

    def half_masks(self):
        return [member * self.tensors for member in range(self.half)]

    def by_part(self, mine, theirs):
        return jnp.where(self.upper, theirs, mine), jnp.where(self.upper, mine, theirs)

    def spread(self, value, masks):
        return [value] + [self.swap(value, mask) for mask in masks[1:]]

    def collect(self, chunks, masks):
        return self.total(self.fetch(chunks, masks))

    def fetch(self, chunks, masks):
        return [chunks[0]] + [
            self.swap(chunk.astype(BF), mask) for chunk, mask in zip(chunks[1:], masks[1:])
        ]

    def total(self, pieces):
        total = pieces[0].astype(F32)
        for piece in pieces[1:]:
            total = total + piece.astype(F32)
        return total

    def exchange_context(self, chunks):
        return lax.all_to_all(chunks, CONTEXT, 0, 0)

    def spread_context(self, value):
        return self.exchange_context(
            jnp.broadcast_to(value[None], (self.contexts, *value.shape))
        )

    def relative(self, slots, index):
        count, shape = slots.shape[0], slots.shape[1:]
        bit = 1
        while bit < count:
            pairs = slots.reshape(count // (2 * bit), 2, bit, *shape)
            flipped = jnp.concatenate([pairs[:, 1:], pairs[:, :1]], axis=1)
            odd = (index // bit) % 2 == 1
            slots = jnp.where(odd, flipped, pairs).reshape(count, *shape)
            bit *= 2
        return slots

    def gather_rows(self, rows):
        return self.gather_square(self.gather_line(rows))

    def gather_line(self, rows):
        return join(self.spread(rows, self.line_masks()))

    def gather_square(self, line):
        own = join(self.spread(line, self.square_masks()))
        return own, self.swap(own, 1)

    def move_start(self, chunks):
        return self.exchange_context(chunks)

    def reduce_start(self, own, other):
        half = own + self.swap(other.astype(BF), 1).astype(F32)
        masks = self.square_masks()
        return self.fetch(jnp.split(half, len(masks), axis=0), masks)

    def reduce_end(self, pieces):
        line = self.total(pieces)
        masks = self.line_masks()
        return self.collect(jnp.split(line, len(masks), axis=0), masks)

    def reduce_rows(self, own, other):
        return self.reduce_end(self.reduce_start(own, other))

    def spread_rows(self, rows):
        stages = []
        for mask in (self.far_half, 2, 1):
            rows = join([rows, self.swap(rows, mask)])
            stages.append(rows)
        return rows, stages[0]

    def return_rows(self, partial):
        for mask in (1, 2, self.far_half):
            own, other = jnp.split(partial, 2, axis=0)
            partial = own + self.swap(other.astype(BF), mask).astype(F32)
        return partial

    def both_parts(self, mine, theirs):
        got = self.swap(theirs, self.far_half)
        joined = join_at([mine[None], got[None]], self.upper.astype(jnp.int32))
        return joined.reshape(2, *mine.shape)

    def gather_half(self, shard, behind):
        if not behind and self.half <= 4:
            return join_at(self.spread(shard, self.half_masks()), self.place)
        return lax.all_gather(
            shard, AXES, axis=1, tiled=True, axis_index_groups=self.half_groups
        )

    def scatter_start(self, partial):
        rows, columns = partial.shape
        partial = partial.reshape(2, rows // 2, columns)
        if self.half > 4:
            return [
                lax.psum_scatter(
                    partial.astype(BF),
                    AXES,
                    scatter_dimension=1,
                    axis_index_groups=self.half_groups,
                    tiled=True,
                )
            ]
        return self.fetch(split_at(partial, self.half, self.place), self.half_masks())

    def scatter_end(self, pieces):
        shard = self.total(pieces).astype(BF)
        mine = jnp.where(self.upper, shard[1], shard[0])
        theirs = jnp.where(self.upper, shard[0], shard[1])
        got = self.swap(theirs, self.far_half)
        return [part.astype(F32) for part in self.by_part(mine, got)]


def body(
    residual_in,
    grad_output,
    block_order,
    w_query,
    key_weight,
    value_weight,
    w_out,
    w_gate,
    w_up,
    w_down,
    attn_gain,
    mlp_gain,
    query_gain,
    key_gain,
):
    contexts, tensors = lax.axis_size(CONTEXT), lax.axis_size(TENSOR)
    links = Links(contexts, tensors)
    masks = links.half_masks()
    layers = w_query.shape[0]
    head_dim = query_gain.shape[1]
    local_rows, width = residual_in.shape
    context_rows = local_rows * tensors
    rows_per_block = context_rows // 2
    all_rows = context_rows * contexts
    key_pos = row_positions(block_order, jnp.int32(0), all_rows, rows_per_block)
    key_pos = links.relative(key_pos.reshape(contexts, context_rows), links.context)
    key_pos = key_pos.reshape(contexts, tensors, local_rows)
    tensor = lax.axis_index(TENSOR)
    key_pos = links.relative(key_pos.transpose(1, 0, 2), tensor)
    key_pos = key_pos.reshape(2, 2, 2, links.half, local_rows).transpose(3, 1, 0, 2, 4)
    key_pos = key_pos.reshape(links.half, 2 * context_rows)
    query_pos = key_pos[0]
    cosine, sine = rotary_tables(query_pos, head_dim)
    tables = (
        jnp.concatenate([cosine, cosine], axis=1),
        jnp.concatenate([-sine, sine], axis=1),
    )
    query_pos = query_pos[:, None]
    query_width, kv_width = w_query.shape[2] // 2, key_weight.shape[2] // 2
    query_heads = query_width // head_dim
    kv_heads = kv_width // head_dim
    units = w_gate.shape[2] // contexts
    shard = w_query.shape[1]
    query_gains = [query_gain[layer][None] for layer in range(layers)]
    key_gains = [key_gain[layer][None] for layer in range(layers)]

    gains = jnp.concatenate([attn_gain, mlp_gain], axis=0)
    gains = links.spread_context(gains).transpose(1, 0, 2).reshape(2 * layers, width)
    gains = gains.astype(F32)

    def ffn_parts(layer):
        parts = [w_gate[layer], w_up[layer], w_down[layer].T]
        parts = [part.reshape(shard, contexts, units) for part in parts]
        parts = [jnp.concatenate(parts[:2], axis=2), parts[2]]
        return [part.transpose(1, 0, 2) for part in parts]

    def move(piece, *others):
        if moves:
            others = (*others, moves[-1])
        piece = after(piece, *others) if others else piece
        moves.append(links.move_start(piece))
        return moves[-1]

    moves = []
    packed = []
    for layer in range(layers):
        packed.append(ffn_parts(layer))
    attn_weights, out_weights = [], []
    ffn_weights = [[None] * 2 for _ in range(layers)]

    def fetch(layer, at, *others):
        ffn_weights[layer][at] = move(packed[layer][at], *others).reshape(width, -1)

    for layer in range(layers):
        parts = []
        for part in range(2):
            query_at = slice(part * query_width, (part + 1) * query_width)
            kv_at = slice(part * kv_width, (part + 1) * kv_width)
            columns = [
                w_query[layer][:, query_at],
                key_weight[layer][:, kv_at],
                value_weight[layer][:, kv_at],
                w_out[layer].T[:, query_at],
            ]
            parts.append(jnp.concatenate(columns, axis=1))
        mine, theirs = links.by_part(*parts)
        cuts = [query_width + 2 * kv_width]
        mine, theirs = jnp.split(mine, cuts, axis=1), jnp.split(theirs, cuts, axis=1)
        if layer:
            held = [links.both_parts(a, b) for a, b in zip(mine, theirs)]
        else:
            taken = links.both_parts(mine[0], theirs[0])
            taken = links.gather_half(taken, False)
            attn_weights.append(taken.reshape(width, -1))
        if not layer:
            taken = links.both_parts(mine[1], theirs[1])
            out_weights.append(links.gather_half(taken, False).reshape(width, -1))

    current = residual_in
    stored = []
    for layer in range(layers):
        gain_attn, gain_mlp = gains[layer], gains[layers + layer]
        normed_in = links.spread_rows(rms_scale(current, gain_attn).astype(BF))[0]
        projected = mm(normed_in, attn_weights[layer])
        pair_proj, query_proj = projected[:, query_width:], projected[:, :query_width]
        pairs = prep_heads(pair_proj, kv_heads, key_gains[layer], tables)
        pairs = links.spread(pairs, masks)
        queries = prep_heads(query_proj, query_heads, query_gains[layer], tables)
        if layer == 0:
            top_gradient = links.gather_rows(after(grad_output, *pairs).astype(BF))
        if layer == 0:
            shards = after(held, *pairs)
            attn_weights.append(links.gather_half(shards[0], True).reshape(width, -1))
        fetch(layer, layer, *pairs)
        output_rows, log_totals = attend(queries, pairs, query_pos, key_pos, head_dim)
        partial = mm_nt(output_rows, out_weights[layer])
        middle = current + links.return_rows(partial)
        line = links.gather_line(rms_scale(middle, gain_mlp).astype(BF))
        if layer == 0:
            fetch(layer, 1, line)
        normed_mid = links.gather_square(line)
        if layer + 1 < layers:
            fetch(layer + 1, 0, normed_mid[0])
        inner, partial = [], []
        weights = ffn_weights[layer]
        for rows in normed_mid:
            both = mm(rows, weights[0])
            gate, up = both[:, :units], both[:, units:]
            hidden = (jax.nn.silu(gate) * up).astype(BF)
            inner.append((gate, up, hidden))
            partial.append(mm_nt(hidden, weights[1]))
        if layer + 1 < layers:
            block_out = middle + links.reduce_rows(*partial)
            taken = links.gather_half(after(shards[1], block_out), True)
            out_weights.append(taken.reshape(width, -1))
        else:
            last = (middle, partial)
        stored.append(
            (
                current,
                normed_in,
                query_proj,
                pair_proj,
                queries,
                pairs,
                output_rows,
                log_totals,
                middle,
                normed_mid,
                inner,
            )
        )
        if layer + 1 < layers:
            current = block_out

    def finish_ffn(pieces, late):
        parts = [
            piece.transpose(1, 0, 2).reshape(shard, -1).astype(F32)
            for piece in after(pieces, late)
        ]
        return parts[0], parts[1], parts[2].T

    def finish_attn(left, lates):
        out_pieces, query_pieces, pair_pieces = [after(a, b) for a, b in zip(left, lates)]
        d_out = jnp.concatenate(links.scatter_end(out_pieces), axis=1).T
        d_query = jnp.concatenate(links.scatter_end(query_pieces), axis=1)
        halves = links.scatter_end(pair_pieces)
        d_key = jnp.concatenate([half[:, :kv_width] for half in halves], axis=1)
        d_value = jnp.concatenate([half[:, kv_width:] for half in halves], axis=1)
        return d_query, d_key, d_value, d_out

    grad_res, moved = grad_output, None
    weight_grads, gain_grads = [None] * layers, [None] * layers
    for layer in reversed(range(layers)):
        (
            layer_in,
            normed_in,
            query_proj,
            pair_proj,
            queries,
            pairs,
            output_rows,
            log_totals,
            middle,
            normed_mid,
            inner,
        ) = stored[layer]
        gain_attn, gain_mlp = gains[layer], gains[layers + layer]
        if layer + 1 == layers:
            grad_all = top_gradient
        else:
            line = links.gather_line(grad_res.astype(BF))
            moved[1] = move(held_grads[1], line)
            grad_all = links.gather_square(line)
            final_pieces = after(final_pieces, grad_all[0])
            final_out = middle_last + links.reduce_end(final_pieces)
            weight_grads[layer + 1] = finish_attn(left, [grad_all[0]] * 3)
        partial, d_in, d_down = [], 0.0, 0.0
        weights = ffn_weights[layer]
        for rows, grad_rows, (gate, up, hidden) in zip(normed_mid, grad_all, inner):
            grad_hidden = mm(grad_rows, weights[1])
            sigmoid = jax.nn.sigmoid(gate)
            grad_up = (grad_hidden * gate * sigmoid).astype(BF)
            grad_gate = (
                grad_hidden * up * sigmoid * (1.0 + gate * (1.0 - sigmoid))
            ).astype(BF)
            both = jnp.concatenate([grad_gate, grad_up], axis=1)
            partial.append(mm_nt(both, weights[0]))
            d_in = d_in + mm_tn(rows, both)
            d_down = d_down + mm_tn(grad_rows, hidden)
        held_grads = [
            grads.astype(BF).reshape(contexts, shard, units)
            for grads in (d_in[:, :units], d_in[:, units:], d_down)
        ]
        last_moved, moved = moved, [None] * 3
        pieces = links.reduce_start(*partial)
        if layer == 0:
            moved[2] = move(held_grads[2], partial[1])
        grad_normed_mid = links.reduce_end(pieces)
        unused, norm_back = jax.vjp(rms_scale, middle, gain_mlp)
        grad_mid_part, d_mlp_gain = norm_back(grad_normed_mid)
        grad_mid = grad_res + grad_mid_part
        grad_mid_all, far_rows = links.spread_rows(grad_mid.astype(BF))
        at = 0 if layer == 0 else 2
        moved[at] = move(held_grads[at], far_rows)
        out_pieces = links.scatter_start(mm_tn(grad_mid_all, output_rows))
        attention_gradient = mm(grad_mid_all, out_weights[layer]).astype(BF)
        if layer + 1 == layers:
            middle_last, partial_last = last
            final_pieces = links.reduce_start(*after(partial_last, grad_mid_all))
        query_grad, pair_grads = attend_back(
            queries,
            pairs,
            query_pos,
            key_pos,
            output_rows,
            log_totals,
            attention_gradient,
            head_dim,
        )
        pair_grads = [pair_grads[0]] + [
            links.swap(grad, mask) for grad, mask in zip(pair_grads[1:], masks[1:])
        ]
        at = 1 if layer == 0 else 0
        moved[at] = move(held_grads[at], *pair_grads)
        if layer == 0:
            weight_grads[1] = (*weight_grads[1], *finish_ffn(last_moved, query_grad))
        grad_queries, d_query_gain = prep_heads_back(
            query_proj, query_heads, query_gains[layer], tables, [query_grad]
        )
        grad_pairs, d_key_gain = prep_heads_back(
            pair_proj, kv_heads, key_gains[layer], tables, pair_grads
        )
        grad_projected = jnp.concatenate([grad_queries, grad_pairs], axis=1)
        partial = mm_nt(grad_projected, attn_weights[layer])
        grad_normed_in = links.return_rows(partial)
        unused, input_back = jax.vjp(rms_scale, layer_in, gain_attn)
        grad_in_part, d_attn_gain = input_back(grad_normed_in)
        grad_res = grad_mid + grad_in_part
        query_pieces = links.scatter_start(mm_tn(normed_in, grad_queries))
        pair_pieces = links.scatter_start(mm_tn(normed_in, grad_pairs))
        left = (out_pieces, query_pieces, pair_pieces)
        if layer == 0:
            weight_grads[0] = (*finish_attn(left, [grad_res] * 3), *finish_ffn(moved, partial))
        gain_grads[layer] = (d_attn_gain, d_mlp_gain, d_query_gain[0], d_key_gain[0])

    wide = jnp.stack([g[0] for g in gain_grads] + [g[1] for g in gain_grads])
    wide = wide.reshape(2 * layers, contexts, shard).transpose(1, 0, 2)
    narrow = jnp.stack([g[2] for g in gain_grads] + [g[3] for g in gain_grads])
    wide = wide.reshape(contexts, 1, 2 * layers * shard)
    narrow = jnp.broadcast_to(
        narrow.reshape(1, 1, 2 * layers * head_dim), (contexts, 1, 2 * layers * head_dim)
    )
    pieces = jnp.concatenate([wide, narrow], axis=2)
    pieces = jnp.broadcast_to(pieces, (contexts, tensors, pieces.shape[2]))
    pieces = after(pieces.reshape(contexts * tensors, -1), moves[-1])
    sums = jnp.sum(lax.all_to_all(pieces, AXES, 0, 0, tiled=True), axis=0)
    wide = sums[: 2 * layers * shard].reshape(2, layers, shard)
    narrow = sums[2 * layers * shard :].reshape(2, layers, head_dim)
    stacked = [jnp.stack([grads[member] for grads in weight_grads]) for member in range(7)]
    return (final_out, grad_res, *stacked, wide[0], wide[1], narrow[0], narrow[1])


def solution(mesh):
    rows = P(AXES, None)
    in_split = P(None, CONTEXT, TENSOR)
    out_split = P(None, TENSOR, CONTEXT)
    gain = P(None, CONTEXT)
    weights = (in_split, in_split, in_split, out_split, in_split, in_split, out_split)
    return jax.shard_map(
        body,
        mesh=mesh,
        in_specs=(rows, rows, P(), *weights, gain, gain, P(), P()),
        out_specs=(rows, rows, *weights, gain, gain, P(), P()),
        check_vma=False,
    )
```

```python
import functools

import jax
import jax.numpy as jnp
from jax import lax
from jax.experimental import pallas as pl
from jax.experimental.pallas import tpu as pltpu
from jax.sharding import PartitionSpec as P

EPSILON = 1e-06
THETA = 1000000.0
CONTEXT, TENSOR = AXES = ("context", "tensor")
BF = jnp.bfloat16
F32 = jnp.float32


def mm(a, b):
    return jnp.dot(a, b, preferred_element_type=F32)


def mm_tn(a, b):
    return lax.dot_general(a, b, (((0,), (0,)), ((), ())), preferred_element_type=F32)


def mm_nt(a, b):
    return lax.dot_general(a, b, (((1,), (1,)), ((), ())), preferred_element_type=F32)


def rms_scale(row_data, gain_row):
    mean_square = jnp.mean(row_data * row_data, axis=-1, keepdims=True)
    return row_data * lax.rsqrt(mean_square + EPSILON) * gain_row


def rotary_tables(positions, head_dim):
    half_dim = head_dim // 2
    exponent = jnp.arange(half_dim, dtype=F32) * (2.0 / head_dim)
    inverse = jnp.power(F32(THETA), -exponent)
    angles = positions.astype(F32)[:, None] * inverse[None, :]
    return (jnp.cos(angles), jnp.sin(angles))


def row_positions(block_order, first_row, row_count, rows_per_block):
    rows_index = first_row + jnp.arange(row_count, dtype=jnp.int32)
    slot_index = rows_index // rows_per_block
    slots = jnp.arange(block_order.shape[0], dtype=jnp.int32)
    matches = slot_index[:, None] == slots[None, :]
    owners = jnp.sum(jnp.where(matches, block_order[None, :], 0), axis=1)
    return owners * rows_per_block + rows_index % rows_per_block


def after(value, *others):
    return lax.optimization_barrier((value, others))[0]


def rows_call(kernel, out_shapes, *operands):
    return pl.pallas_call(
        kernel,
        out_shape=[jax.ShapeDtypeStruct(shape, kind) for shape, kind in out_shapes],
        compiler_params=pltpu.CompilerParams(vmem_limit_bytes=48 * 1024 * 1024),
    )(*operands)


def join_kernel(*refs):
    *pieces, out_ref = refs
    count = pieces[0].shape[0]
    for slot, piece in enumerate(pieces):
        out_ref[slot * count : (slot + 1) * count, :] = piece[...]


def join(pieces):
    rows, width = pieces[0].shape
    return rows_call(join_kernel, [((len(pieces) * rows, width), pieces[0].dtype)], *pieces)[0]


def index_call(kernel, out_shapes, index, *operands):
    vmem = pl.BlockSpec(memory_space=pltpu.VMEM)
    return pl.pallas_call(
        kernel,
        in_specs=[pl.BlockSpec(memory_space=pltpu.SMEM)] + [vmem] * len(operands),
        out_specs=[vmem] * len(out_shapes),
        out_shape=[jax.ShapeDtypeStruct(shape, kind) for shape, kind in out_shapes],
        compiler_params=pltpu.CompilerParams(vmem_limit_bytes=48 * 1024 * 1024),
    )(index.reshape(1), *operands)


def join_at_kernel(index_ref, *refs):
    *pieces, out_ref = refs
    count = pieces[0].shape[1]
    for slot, piece in enumerate(pieces):
        first = pl.multiple_of((index_ref[0] ^ slot) * count, count)
        out_ref[:, pl.ds(first, count), :] = piece[...]


def join_at(pieces, index):
    parts, rows, width = pieces[0].shape
    shape = (parts, len(pieces) * rows, width)
    return index_call(join_at_kernel, [(shape, pieces[0].dtype)], index, *pieces)[0]


def split_at_kernel(index_ref, x_ref, *outs):
    count = outs[0].shape[1]
    for slot, out in enumerate(outs):
        first = pl.multiple_of((index_ref[0] ^ slot) * count, count)
        out[...] = x_ref[:, pl.ds(first, count), :].astype(out.dtype)


def split_at(x, places, index, own=F32):
    parts, rows, width = x.shape
    shape = (parts, rows // places, width)
    shapes = [(shape, BF if slot else own) for slot in range(places)]
    return index_call(split_at_kernel, shapes, index, x)


def prep_kernel(heads, x_ref, gain_ref, cos_ref, sin_ref, out_ref):
    head_dim = gain_ref.shape[1]
    for head in range(x_ref.shape[1] // head_dim):
        at = slice(head * head_dim, (head + 1) * head_dim)
        rows = x_ref[:, at]
        if head < heads:
            mean_square = jnp.mean(rows * rows, axis=-1, keepdims=True)
            rows = rows * lax.rsqrt(mean_square + EPSILON) * gain_ref[...]
            rows = rows * cos_ref[...] + pltpu.roll(rows, head_dim // 2, 1) * sin_ref[...]
        out_ref[:, at] = rows.astype(BF)


def prep_heads(projected, heads, gain, tables):
    kernel = functools.partial(prep_kernel, heads)
    return rows_call(kernel, [(projected.shape, BF)], projected, gain, *tables)[0]


def prep_back_kernel(heads, x_ref, gain_ref, cos_ref, sin_ref, *refs):
    grads, (out_ref, gain_grad_ref) = refs[:-2], refs[-2:]
    head_dim = gain_ref.shape[1]
    gain_grad = jnp.zeros((1, head_dim), F32)
    for head in range(x_ref.shape[1] // head_dim):
        at = slice(head * head_dim, (head + 1) * head_dim)
        grad = grads[0][:, at].astype(F32)
        for piece in grads[1:]:
            grad = grad + piece[:, at].astype(F32)
        if head < heads:
            rows = x_ref[:, at]
            mean_square = jnp.mean(rows * rows, axis=-1, keepdims=True)
            scale = lax.rsqrt(mean_square + EPSILON)
            unit = rows * scale
            grad = grad * cos_ref[...] + pltpu.roll(grad * sin_ref[...], head_dim // 2, 1)
            gain_grad = gain_grad + jnp.sum(grad * unit, axis=0, keepdims=True)
            grad = grad * gain_ref[...]
            grad = scale * (grad - unit * jnp.mean(grad * unit, axis=-1, keepdims=True))
        out_ref[:, at] = grad.astype(BF)
    gain_grad_ref[...] = gain_grad


def prep_heads_back(projected, heads, gain, tables, grads):
    kernel = functools.partial(prep_back_kernel, heads)
    shapes = [(projected.shape, BF), (gain.shape, F32)]
    return rows_call(kernel, shapes, projected, gain, *tables, *grads)


def dot_nt(a, b):
    return lax.dot_general(a, b, (((1,), (1,)), ((), ())), preferred_element_type=F32)


def dot_tn(a, b):
    return lax.dot_general(a, b, (((0,), (0,)), ((), ())), preferred_element_type=F32)


def stack_heads(ref, first, groups, head_dim):
    return jnp.concatenate(
        [ref[:, (first + i) * head_dim : (first + i + 1) * head_dim] for i in range(groups)], axis=0
    )


def attend_kernel(head_dim, query_ref, query_pos_ref, key_pos_ref, *refs):
    pairs, (out_ref, log_ref) = refs[:-2], refs[-2:]
    count = query_ref.shape[0]
    kv_heads = pairs[0].shape[1] // (2 * head_dim)
    groups = query_ref.shape[1] // (kv_heads * head_dim)
    query_pos = jnp.concatenate([query_pos_ref[...]] * groups, axis=0)
    for kv_head in range(kv_heads):
        queries = stack_heads(query_ref, kv_head * groups, groups, head_dim)
        totals = jnp.zeros((groups * count, 1), F32)
        summed = jnp.zeros((groups * count, head_dim), F32)
        for slot, pair in enumerate(pairs):
            keys = pair[:, kv_head * head_dim : (kv_head + 1) * head_dim]
            values = pair[:, (kv_heads + kv_head) * head_dim : (kv_heads + kv_head + 1) * head_dim]
            scores = dot_nt(queries, keys) * head_dim ** (-0.5)
            causal = key_pos_ref[slot : slot + 1, :] <= query_pos
            weights = jnp.where(causal, jnp.exp(scores), 0.0)
            totals = totals + jnp.sum(weights, axis=-1, keepdims=True)
            summed = summed + jnp.dot(weights.astype(BF), values, preferred_element_type=F32)
        outputs = summed / totals
        logs = jnp.log(totals)
        for group in range(groups):
            head = kv_head * groups + group
            at = slice(group * count, (group + 1) * count)
            out_ref[:, head * head_dim : (head + 1) * head_dim] = outputs[at].astype(BF)
            log_ref[:, head : head + 1] = logs[at]


def attend(queries, pairs, query_pos, key_pos, head_dim):
    heads = queries.shape[1] // head_dim
    shapes = [(queries.shape, BF), ((queries.shape[0], heads), F32)]
    kernel = functools.partial(attend_kernel, head_dim)
    return rows_call(kernel, shapes, queries, query_pos, key_pos, *pairs)


def attend_back_kernel(
    head_dim, query_ref, query_pos_ref, key_pos_ref, out_ref, log_ref, grad_ref, *refs
):
    slots = (len(refs) - 1) // 2
    pairs, query_grad_ref, pair_grads = refs[:slots], refs[slots], refs[slots + 1 :]
    count = query_ref.shape[0]
    scale = head_dim ** (-0.5)
    kv_heads = pairs[0].shape[1] // (2 * head_dim)
    groups = query_ref.shape[1] // (kv_heads * head_dim)
    query_pos = jnp.concatenate([query_pos_ref[...]] * groups, axis=0)
    for kv_head in range(kv_heads):
        first = kv_head * groups
        queries = stack_heads(query_ref, first, groups, head_dim)
        grads = stack_heads(grad_ref, first, groups, head_dim)
        outputs = stack_heads(out_ref, first, groups, head_dim)
        logs = jnp.concatenate(
            [log_ref[:, first + i : first + i + 1] for i in range(groups)], axis=0
        )
        deltas = jnp.sum(grads.astype(F32) * outputs.astype(F32), axis=-1, keepdims=True)
        query_grad = jnp.zeros((groups * count, head_dim), F32)
        key_at = slice(kv_head * head_dim, (kv_head + 1) * head_dim)
        value_at = slice((kv_heads + kv_head) * head_dim, (kv_heads + kv_head + 1) * head_dim)
        for slot in range(slots):
            keys, values = pairs[slot][:, key_at], pairs[slot][:, value_at]
            scores = dot_nt(queries, keys) * scale
            causal = key_pos_ref[slot : slot + 1, :] <= query_pos
            probs = jnp.where(causal, jnp.exp(scores - logs), 0.0)
            value_grad = dot_tn(probs.astype(BF), grads)
            grad_probs = dot_nt(grads, values)
            grad_scores = (probs * (grad_probs - deltas) * scale).astype(BF)
            query_grad = query_grad + jnp.dot(grad_scores, keys, preferred_element_type=F32)
            key_grad = dot_tn(grad_scores, queries)
            pair_grads[slot][:, key_at] = key_grad.astype(pair_grads[slot].dtype)
            pair_grads[slot][:, value_at] = value_grad.astype(pair_grads[slot].dtype)
        for group in range(groups):
            head = first + group
            query_grad_ref[:, head * head_dim : (head + 1) * head_dim] = query_grad[
                group * count : (group + 1) * count
            ]


def attend_back(queries, pairs, query_pos, key_pos, outputs, logs, grads, head_dim):
    kernel = functools.partial(attend_back_kernel, head_dim)
    shapes = [(queries.shape, F32)]
    shapes += [(pair.shape, BF if slot else F32) for slot, pair in enumerate(pairs)]
    query_grad, *pair_grads = rows_call(
        kernel, shapes, queries, query_pos, key_pos, outputs, logs, grads, *pairs
    )
    return query_grad, pair_grads


class Links:
    def __init__(self, contexts, tensors):
        self.contexts, self.tensors = contexts, tensors
        self.count = contexts * tensors
        self.half = contexts // 2
        self.far_half = self.half * tensors
        self.half_groups = [
            [(part * self.half + member) * tensors + tensor for member in range(self.half)]
            for part in range(2)
            for tensor in range(tensors)
        ]
        self.context = lax.axis_index(CONTEXT)
        self.upper = self.context >= self.half
        self.place = self.context % self.half

    def swap(self, value, mask):
        return lax.ppermute(value, AXES, [(i, i ^ mask) for i in range(self.count)])

    def line_masks(self):
        return [2 * place * self.tensors for place in range(self.half)]

    def square_masks(self):
        return [
            side * self.tensors + row * 2 for side in range(2) for row in range(self.tensors // 2)
        ]

    def half_masks(self):
        return [member * self.tensors for member in range(self.half)]

    def by_part(self, mine, theirs):
        return jnp.where(self.upper, theirs, mine), jnp.where(self.upper, mine, theirs)

    def spread(self, value, masks):
        return [value] + [self.swap(value, mask) for mask in masks[1:]]

    def collect(self, chunks, masks):
        return self.total(self.fetch(chunks, masks))

    def fetch(self, chunks, masks):
        return [chunks[0]] + [
            self.swap(chunk.astype(BF), mask) for chunk, mask in zip(chunks[1:], masks[1:])
        ]

    def total(self, pieces):
        total = pieces[0].astype(F32)
        for piece in pieces[1:]:
            total = total + piece.astype(F32)
        return total

    def exchange_context(self, chunks):
        return lax.all_to_all(chunks, CONTEXT, 0, 0)

    def spread_context(self, value):
        return self.exchange_context(
            jnp.broadcast_to(value[None], (self.contexts, *value.shape))
        )

    def relative(self, slots, index):
        count, shape = slots.shape[0], slots.shape[1:]
        bit = 1
        while bit < count:
            pairs = slots.reshape(count // (2 * bit), 2, bit, *shape)
            flipped = jnp.concatenate([pairs[:, 1:], pairs[:, :1]], axis=1)
            odd = (index // bit) % 2 == 1
            slots = jnp.where(odd, flipped, pairs).reshape(count, *shape)
            bit *= 2
        return slots

    def gather_rows(self, rows):
        return self.gather_square(self.gather_line(rows))

    def gather_line(self, rows):
        return join(self.spread(rows, self.line_masks()))

    def gather_square(self, line):
        own = join(self.spread(line, self.square_masks()))
        return own, self.swap(own, 1)

    def move_start(self, chunks):
        return self.exchange_context(chunks)

    def reduce_start(self, own, other):
        half = own + self.swap(other.astype(BF), 1).astype(F32)
        masks = self.square_masks()
        return self.fetch(jnp.split(half, len(masks), axis=0), masks)

    def reduce_end(self, pieces):
        line = self.total(pieces)
        masks = self.line_masks()
        return self.collect(jnp.split(line, len(masks), axis=0), masks)

    def reduce_rows(self, own, other):
        return self.reduce_end(self.reduce_start(own, other))

    def spread_rows(self, rows):
        for mask in (self.far_half, 2, 1):
            rows = join([rows, self.swap(rows, mask)])
        return rows

    def return_rows(self, partial):
        for mask in (1, 2, self.far_half):
            own, other = jnp.split(partial, 2, axis=0)
            partial = own + self.swap(other.astype(BF), mask).astype(F32)
        return partial

    def both_parts(self, mine, theirs):
        got = self.swap(theirs, self.far_half)
        joined = join_at([mine[None], got[None]], self.upper.astype(jnp.int32))
        return joined.reshape(2, *mine.shape)

    def gather_half(self, shard, behind):
        if not behind and self.half <= 4:
            return join_at(self.spread(shard, self.half_masks()), self.place)
        return lax.all_gather(
            shard, AXES, axis=1, tiled=True, axis_index_groups=self.half_groups
        )

    def scatter_start(self, partial):
        rows, columns = partial.shape
        partial = partial.reshape(2, rows // 2, columns)
        if self.half > 4:
            return [
                lax.psum_scatter(
                    partial.astype(BF),
                    AXES,
                    scatter_dimension=1,
                    axis_index_groups=self.half_groups,
                    tiled=True,
                )
            ]
        return self.fetch(split_at(partial, self.half, self.place), self.half_masks())

    def scatter_end(self, pieces):
        shard = self.total(pieces).astype(BF)
        mine = jnp.where(self.upper, shard[1], shard[0])
        theirs = jnp.where(self.upper, shard[0], shard[1])
        got = self.swap(theirs, self.far_half)
        return [part.astype(F32) for part in self.by_part(mine, got)]


def body(
    residual_in,
    grad_output,
    block_order,
    w_query,
    key_weight,
    value_weight,
    w_out,
    w_gate,
    w_up,
    w_down,
    attn_gain,
    mlp_gain,
    query_gain,
    key_gain,
):
    contexts, tensors = lax.axis_size(CONTEXT), lax.axis_size(TENSOR)
    links = Links(contexts, tensors)
    masks = links.half_masks()
    layers = w_query.shape[0]
    head_dim = query_gain.shape[1]
    local_rows, width = residual_in.shape
    context_rows = local_rows * tensors
    rows_per_block = context_rows // 2
    all_rows = context_rows * contexts
    key_pos = row_positions(block_order, jnp.int32(0), all_rows, rows_per_block)
    key_pos = links.relative(key_pos.reshape(contexts, context_rows), links.context)
    key_pos = key_pos.reshape(contexts, tensors, local_rows)
    tensor = lax.axis_index(TENSOR)
    key_pos = links.relative(key_pos.transpose(1, 0, 2), tensor)
    key_pos = key_pos.reshape(2, 2, 2, links.half, local_rows).transpose(3, 1, 0, 2, 4)
    key_pos = key_pos.reshape(links.half, 2 * context_rows)
    query_pos = key_pos[0]
    cosine, sine = rotary_tables(query_pos, head_dim)
    tables = (
        jnp.concatenate([cosine, cosine], axis=1),
        jnp.concatenate([-sine, sine], axis=1),
    )
    query_pos = query_pos[:, None]
    query_width, kv_width = w_query.shape[2] // 2, key_weight.shape[2] // 2
    query_heads = query_width // head_dim
    kv_heads = kv_width // head_dim
    units = w_gate.shape[2] // contexts
    shard = w_query.shape[1]
    query_gains = [query_gain[layer][None] for layer in range(layers)]
    key_gains = [key_gain[layer][None] for layer in range(layers)]

    gains = jnp.concatenate([attn_gain, mlp_gain], axis=0)
    gains = links.spread_context(gains).transpose(1, 0, 2).reshape(2 * layers, width)
    gains = gains.astype(F32)

    def ffn_parts(layer):
        parts = [w_gate[layer], w_up[layer], w_down[layer].T]
        parts = [part.reshape(shard, contexts, units) for part in parts]
        if layer:
            parts = [jnp.concatenate(parts[:2], axis=2), parts[2]]
        return [part.transpose(1, 0, 2) for part in parts]

    packed = []
    for layer in range(layers):
        packed.append(ffn_parts(layer))
    attn_weights, out_weights = [], []
    ffn_weights = [[] for _ in range(layers)]

    def fetch(layer):
        at = len(ffn_weights[layer])
        piece = links.move_start(packed[layer][at])
        ffn_weights[layer].append(piece.reshape(width, -1))

    fetch(0)
    for layer in range(layers):
        parts = []
        for part in range(2):
            query_at = slice(part * query_width, (part + 1) * query_width)
            kv_at = slice(part * kv_width, (part + 1) * kv_width)
            columns = [
                w_query[layer][:, query_at],
                key_weight[layer][:, kv_at],
                value_weight[layer][:, kv_at],
                w_out[layer].T[:, query_at],
            ]
            parts.append(jnp.concatenate(columns, axis=1))
        mine, theirs = links.by_part(*parts)
        cuts = [query_width, query_width + 2 * kv_width] if layer else [query_width + 2 * kv_width]
        mine, theirs = jnp.split(mine, cuts, axis=1), jnp.split(theirs, cuts, axis=1)
        if layer:
            held = [links.both_parts(a, b) for a, b in zip(mine, theirs)]
        else:
            taken = links.both_parts(mine[0], theirs[0])
            taken = links.gather_half(taken, False)
            attn_weights.append(taken.reshape(width, -1))
        if not layer:
            taken = links.both_parts(mine[1], theirs[1])
            out_weights.append(links.gather_half(taken, False).reshape(width, -1))

    current = residual_in
    stored = []
    for layer in range(layers):
        gain_attn, gain_mlp = gains[layer], gains[layers + layer]
        normed_in = links.spread_rows(rms_scale(current, gain_attn).astype(BF))
        if layer:
            query_proj, pair_proj = [mm(normed_in, w) for w in attn_weights[layer]]
        else:
            projected = mm(normed_in, attn_weights[layer])
            query_proj, pair_proj = projected[:, :query_width], projected[:, query_width:]
        pairs = prep_heads(pair_proj, kv_heads, key_gains[layer], tables)
        pairs = links.spread(pairs, masks)
        queries = prep_heads(query_proj, query_heads, query_gains[layer], tables)
        if layer == 0:
            top_gradient = links.gather_rows(after(grad_output, *pairs).astype(BF))
        if layer == 0:
            out_weights.append(links.gather_half(held[2], True).reshape(width, -1))
        fetch(layer)
        output_rows, log_totals = attend(queries, pairs, query_pos, key_pos, head_dim)
        partial = mm_nt(output_rows, out_weights[layer])
        middle = current + links.return_rows(partial)
        line = links.gather_line(rms_scale(middle, gain_mlp).astype(BF))
        if layer == 0:
            fetch(0)
        normed_mid = links.gather_square(line)
        if layer + 1 < layers:
            fetch(layer + 1)
        inner, partial = [], []
        weights = ffn_weights[layer]
        if len(weights) == 3:
            weights[:2] = [jnp.concatenate(weights[:2], axis=1)]
        for rows in normed_mid:
            both = mm(rows, weights[0])
            gate, up = both[:, :units], both[:, units:]
            hidden = (jax.nn.silu(gate) * up).astype(BF)
            inner.append((gate, up, hidden))
            partial.append(mm_nt(hidden, weights[1]))
        if layer + 1 < layers:
            block_out = middle + links.reduce_rows(*partial)
            next_pairs = links.gather_half(held[1], True).reshape(width, -1)
            next_queries = links.gather_half(held[0], True).reshape(width, -1)
            attn_weights.append((next_queries, next_pairs))
        else:
            last = (middle, (partial[0], partial[1].astype(BF)))
        stored.append(
            (
                current,
                normed_in,
                query_proj,
                pair_proj,
                queries,
                pairs,
                output_rows,
                log_totals,
                middle,
                normed_mid,
                inner,
            )
        )
        if layer + 1 < layers:
            current = block_out

    def finish_ffn(pieces, late):
        parts = [
            piece.transpose(1, 0, 2).reshape(shard, -1).astype(F32)
            for piece in after(pieces, late)
        ]
        return parts[0], parts[1], parts[2].T

    def finish_attn(left, late):
        out_pieces, *projected = after(left, late)
        d_out = jnp.concatenate(links.scatter_end(out_pieces), axis=1).T
        shards = [links.scatter_end(pieces) for pieces in projected]
        halves = [jnp.concatenate(pair, axis=1) for pair in zip(*shards)]
        cuts = [query_width, query_width + kv_width]
        d_query, d_key, d_value = [
            jnp.concatenate(pair, axis=1)
            for pair in zip(*[jnp.split(half, cuts, axis=1) for half in halves])
        ]
        return d_query, d_key, d_value, d_out

    grad_res, moved = grad_output, None
    weight_grads, gain_grads = [None] * layers, [None] * layers
    for layer in reversed(range(layers)):
        (
            layer_in,
            normed_in,
            query_proj,
            pair_proj,
            queries,
            pairs,
            output_rows,
            log_totals,
            middle,
            normed_mid,
            inner,
        ) = stored[layer]
        gain_attn, gain_mlp = gains[layer], gains[layers + layer]
        if layer + 1 == layers:
            grad_all = top_gradient
        else:
            line = links.gather_line(grad_res.astype(BF))
            moved[1] = links.move_start(held_grads[1])
            grad_all = links.gather_square(line)
            final_pieces = after(final_pieces, line)
            final_out = middle_last + links.reduce_end(final_pieces)
            weight_grads[layer + 1] = finish_attn(left, line)
        partial, d_in, d_down = [], 0.0, 0.0
        weights = ffn_weights[layer]
        for rows, grad_rows, (gate, up, hidden) in zip(normed_mid, grad_all, inner):
            grad_hidden = mm(grad_rows, weights[1])
            sigmoid = jax.nn.sigmoid(gate)
            grad_up = (grad_hidden * gate * sigmoid).astype(BF)
            grad_gate = (
                grad_hidden * up * sigmoid * (1.0 + gate * (1.0 - sigmoid))
            ).astype(BF)
            both = jnp.concatenate([grad_gate, grad_up], axis=1)
            partial.append(mm_nt(both, weights[0]))
            d_in = d_in + mm_tn(rows, both)
            d_down = d_down + mm_tn(grad_rows, hidden)
        held_grads = [
            grads.astype(BF).reshape(contexts, shard, units)
            for grads in (d_in[:, :units], d_in[:, units:], d_down)
        ]
        last_moved, moved = moved, [None] * 3
        pieces = links.reduce_start(*partial)
        if layer == 0:
            moved[2] = links.move_start(held_grads[2])
        grad_normed_mid = links.reduce_end(pieces)
        unused, norm_back = jax.vjp(rms_scale, middle, gain_mlp)
        grad_mid_part, d_mlp_gain = norm_back(grad_normed_mid)
        grad_mid = grad_res + grad_mid_part
        grad_mid_all = links.spread_rows(grad_mid.astype(BF))
        at = 0 if layer == 0 else 2
        moved[at] = links.move_start(held_grads[at])
        out_pieces = links.scatter_start(mm_tn(grad_mid_all, output_rows))
        attention_gradient = mm(grad_mid_all, out_weights[layer]).astype(BF)
        if layer + 1 == layers:
            middle_last, partial_last = last
            final_pieces = links.reduce_start(*after(partial_last, grad_mid_all))
        query_grad, pair_grads = attend_back(
            queries,
            pairs,
            query_pos,
            key_pos,
            output_rows,
            log_totals,
            attention_gradient,
            head_dim,
        )
        pair_grads = [pair_grads[0]] + [
            links.swap(grad, mask) for grad, mask in zip(pair_grads[1:], masks[1:])
        ]
        at = 1 if layer == 0 else 0
        moved[at] = links.move_start(held_grads[at])
        if layer == 0:
            weight_grads[1] = (*weight_grads[1], *finish_ffn(last_moved, query_grad))
        grad_queries, d_query_gain = prep_heads_back(
            query_proj, query_heads, query_gains[layer], tables, [query_grad]
        )
        grad_pairs, d_key_gain = prep_heads_back(
            pair_proj, kv_heads, key_gains[layer], tables, pair_grads
        )
        if layer:
            partial = mm_nt(grad_queries, attn_weights[layer][0])
            partial = partial + mm_nt(grad_pairs, attn_weights[layer][1])
        else:
            grad_projected = jnp.concatenate([grad_queries, grad_pairs], axis=1)
            partial = mm_nt(grad_projected, attn_weights[layer])
        grad_normed_in = links.return_rows(partial)
        unused, input_back = jax.vjp(rms_scale, layer_in, gain_attn)
        grad_in_part, d_attn_gain = input_back(grad_normed_in)
        grad_res = grad_mid + grad_in_part
        projected = []
        for grads in (grad_queries, grad_pairs):
            projected.append(links.scatter_start(mm_tn(normed_in, grads)))
        left = (out_pieces, *projected)
        if layer == 0:
            weight_grads[0] = (*finish_attn(left, grad_res), *finish_ffn(moved, partial))
        gain_grads[layer] = (d_attn_gain, d_mlp_gain, d_query_gain[0], d_key_gain[0])

    wide = jnp.stack([g[0] for g in gain_grads] + [g[1] for g in gain_grads])
    wide = wide.reshape(2 * layers, contexts, shard).transpose(1, 0, 2)
    narrow = jnp.stack([g[2] for g in gain_grads] + [g[3] for g in gain_grads])
    wide = wide.reshape(contexts, 1, 2 * layers * shard)
    narrow = jnp.broadcast_to(
        narrow.reshape(1, 1, 2 * layers * head_dim), (contexts, 1, 2 * layers * head_dim)
    )
    pieces = jnp.concatenate([wide, narrow], axis=2)
    pieces = jnp.broadcast_to(pieces, (contexts, tensors, pieces.shape[2]))
    pieces = pieces.reshape(contexts * tensors, -1)
    sums = jnp.sum(lax.all_to_all(pieces, AXES, 0, 0, tiled=True), axis=0)
    wide = sums[: 2 * layers * shard].reshape(2, layers, shard)
    narrow = sums[2 * layers * shard :].reshape(2, layers, head_dim)
    stacked = []
    for member in range(7):
        stacked.append(jnp.stack([grads[member] for grads in weight_grads]))
    return (final_out, grad_res, *stacked, wide[0], wide[1], narrow[0], narrow[1])


def solution(mesh):
    rows = P(AXES, None)
    in_split = P(None, CONTEXT, TENSOR)
    out_split = P(None, TENSOR, CONTEXT)
    gain = P(None, CONTEXT)
    weights = (in_split, in_split, in_split, out_split, in_split, in_split, out_split)
    return jax.shard_map(
        body,
        mesh=mesh,
        in_specs=(rows, rows, P(), *weights, gain, gain, P(), P()),
        out_specs=(rows, rows, *weights, gain, gain, P(), P()),
        check_vma=False,
    )
```

```python
import functools

import jax
import jax.numpy as jnp
from jax import lax
from jax.experimental import pallas as pl
from jax.experimental.pallas import tpu as pltpu
from jax.sharding import PartitionSpec as P

EPSILON = 1e-06
THETA = 1000000.0
CONTEXT, TENSOR = AXES = ("context", "tensor")
BF = jnp.bfloat16
F32 = jnp.float32


def mm(a, b):
    return jnp.dot(a, b, preferred_element_type=F32)


def mm_tn(a, b):
    return lax.dot_general(a, b, (((0,), (0,)), ((), ())), preferred_element_type=F32)


def mm_nt(a, b):
    return lax.dot_general(a, b, (((1,), (1,)), ((), ())), preferred_element_type=F32)


def rms_scale(row_data, gain_row):
    mean_square = jnp.mean(row_data * row_data, axis=-1, keepdims=True)
    return row_data * lax.rsqrt(mean_square + EPSILON) * gain_row


def rotary_tables(positions, head_dim):
    half_dim = head_dim // 2
    exponent = jnp.arange(half_dim, dtype=F32) * (2.0 / head_dim)
    inverse = jnp.power(F32(THETA), -exponent)
    angles = positions.astype(F32)[:, None] * inverse[None, :]
    return (jnp.cos(angles), jnp.sin(angles))


def row_positions(block_order, first_row, row_count, rows_per_block):
    rows_index = first_row + jnp.arange(row_count, dtype=jnp.int32)
    slot_index = rows_index // rows_per_block
    slots = jnp.arange(block_order.shape[0], dtype=jnp.int32)
    matches = slot_index[:, None] == slots[None, :]
    owners = jnp.sum(jnp.where(matches, block_order[None, :], 0), axis=1)
    return owners * rows_per_block + rows_index % rows_per_block


def after(value, *others):
    return lax.optimization_barrier((value, others))[0]


def rows_call(kernel, out_shapes, *operands):
    return pl.pallas_call(
        kernel,
        out_shape=[jax.ShapeDtypeStruct(shape, kind) for shape, kind in out_shapes],
        compiler_params=pltpu.CompilerParams(vmem_limit_bytes=48 * 1024 * 1024),
    )(*operands)


def join_kernel(*refs):
    *pieces, out_ref = refs
    count = pieces[0].shape[0]
    for slot, piece in enumerate(pieces):
        out_ref[slot * count : (slot + 1) * count, :] = piece[...]


def join(pieces):
    rows, width = pieces[0].shape
    return rows_call(join_kernel, [((len(pieces) * rows, width), pieces[0].dtype)], *pieces)[0]


def index_call(kernel, out_shapes, index, *operands):
    vmem = pl.BlockSpec(memory_space=pltpu.VMEM)
    return pl.pallas_call(
        kernel,
        in_specs=[pl.BlockSpec(memory_space=pltpu.SMEM)] + [vmem] * len(operands),
        out_specs=[vmem] * len(out_shapes),
        out_shape=[jax.ShapeDtypeStruct(shape, kind) for shape, kind in out_shapes],
        compiler_params=pltpu.CompilerParams(vmem_limit_bytes=48 * 1024 * 1024),
    )(index.reshape(1), *operands)


def join_at_kernel(index_ref, *refs):
    *pieces, out_ref = refs
    count = pieces[0].shape[1]
    for slot, piece in enumerate(pieces):
        first = pl.multiple_of((index_ref[0] ^ slot) * count, count)
        out_ref[:, pl.ds(first, count), :] = piece[...]


def join_at(pieces, index):
    parts, rows, width = pieces[0].shape
    shape = (parts, len(pieces) * rows, width)
    return index_call(join_at_kernel, [(shape, pieces[0].dtype)], index, *pieces)[0]


def split_at_kernel(index_ref, x_ref, *outs):
    count = outs[0].shape[1]
    for slot, out in enumerate(outs):
        first = pl.multiple_of((index_ref[0] ^ slot) * count, count)
        out[...] = x_ref[:, pl.ds(first, count), :].astype(out.dtype)


def split_at(x, places, index, own=F32):
    parts, rows, width = x.shape
    shape = (parts, rows // places, width)
    shapes = [(shape, BF if slot else own) for slot in range(places)]
    return index_call(split_at_kernel, shapes, index, x)


def pack_kernel(layer, gate_ref, up_ref, *outs):
    slots, rows, width = outs[0].shape
    units = width // 2
    for part, out in enumerate(outs):
        row_at = slice(part * rows, (part + 1) * rows)
        gate = gate_ref[layer, row_at, :].astype(F32)
        up = up_ref[layer, row_at, :].astype(F32)
        for slot in range(slots):
            at = slice(slot * units, (slot + 1) * units)
            out[slot, :, :units] = gate[:, at].astype(BF)
            out[slot, :, units:] = up[:, at].astype(BF)


def pack(w_gate, w_up, layer, slots, parts):
    rows, columns = w_gate.shape[1:]
    shapes = [((slots, rows // parts, 2 * columns // slots), BF)] * parts
    return rows_call(functools.partial(pack_kernel, layer), shapes, w_gate, w_up)


def unpack_kernel(*refs):
    *layers, gate_ref, up_ref = refs
    for layer, pieces in enumerate(layers):
        count, _, width = pieces.shape
        units = width // 2
        for slot in range(count):
            at = slice(slot * units, (slot + 1) * units)
            both = pieces[slot].astype(F32)
            gate_ref[layer, :, at] = both[:, :units]
            up_ref[layer, :, at] = both[:, units:]


def unpack(layers):
    count, rows, width = layers[0].shape
    shape = (len(layers), rows, count * width // 2)
    return rows_call(unpack_kernel, [(shape, F32)] * 2, *layers)


def prep_kernel(heads, x_ref, gain_ref, cos_ref, sin_ref, out_ref):
    head_dim = gain_ref.shape[1]
    for head in range(x_ref.shape[1] // head_dim):
        at = slice(head * head_dim, (head + 1) * head_dim)
        rows = x_ref[:, at]
        if head < heads:
            mean_square = jnp.mean(rows * rows, axis=-1, keepdims=True)
            rows = rows * lax.rsqrt(mean_square + EPSILON) * gain_ref[...]
            rows = rows * cos_ref[...] + pltpu.roll(rows, head_dim // 2, 1) * sin_ref[...]
        out_ref[:, at] = rows.astype(BF)


def prep_heads(projected, heads, gain, tables):
    kernel = functools.partial(prep_kernel, heads)
    return rows_call(kernel, [(projected.shape, BF)], projected, gain, *tables)[0]


def prep_back_kernel(heads, x_ref, gain_ref, cos_ref, sin_ref, *refs):
    grads, (out_ref, gain_grad_ref) = refs[:-2], refs[-2:]
    head_dim = gain_ref.shape[1]
    gain_grad = jnp.zeros((1, head_dim), F32)
    for head in range(x_ref.shape[1] // head_dim):
        at = slice(head * head_dim, (head + 1) * head_dim)
        grad = grads[0][:, at].astype(F32)
        for piece in grads[1:]:
            grad = grad + piece[:, at].astype(F32)
        if head < heads:
            rows = x_ref[:, at]
            mean_square = jnp.mean(rows * rows, axis=-1, keepdims=True)
            scale = lax.rsqrt(mean_square + EPSILON)
            unit = rows * scale
            grad = grad * cos_ref[...] + pltpu.roll(grad * sin_ref[...], head_dim // 2, 1)
            gain_grad = gain_grad + jnp.sum(grad * unit, axis=0, keepdims=True)
            grad = grad * gain_ref[...]
            grad = scale * (grad - unit * jnp.mean(grad * unit, axis=-1, keepdims=True))
        out_ref[:, at] = grad.astype(BF)
    gain_grad_ref[...] = gain_grad


def prep_heads_back(projected, heads, gain, tables, grads):
    kernel = functools.partial(prep_back_kernel, heads)
    shapes = [(projected.shape, BF), (gain.shape, F32)]
    return rows_call(kernel, shapes, projected, gain, *tables, *grads)


def dot_nt(a, b):
    return lax.dot_general(a, b, (((1,), (1,)), ((), ())), preferred_element_type=F32)


def dot_tn(a, b):
    return lax.dot_general(a, b, (((0,), (0,)), ((), ())), preferred_element_type=F32)


def stack_heads(ref, first, groups, head_dim):
    return jnp.concatenate(
        [ref[:, (first + i) * head_dim : (first + i + 1) * head_dim] for i in range(groups)], axis=0
    )


def attend_kernel(head_dim, query_ref, query_pos_ref, key_pos_ref, *refs):
    pairs, (out_ref, log_ref) = refs[:-2], refs[-2:]
    count = query_ref.shape[0]
    kv_heads = pairs[0].shape[1] // (2 * head_dim)
    groups = query_ref.shape[1] // (kv_heads * head_dim)
    query_pos = jnp.concatenate([query_pos_ref[...]] * groups, axis=0)
    for kv_head in range(kv_heads):
        queries = stack_heads(query_ref, kv_head * groups, groups, head_dim)
        totals = jnp.zeros((groups * count, 1), F32)
        summed = jnp.zeros((groups * count, head_dim), F32)
        for slot, pair in enumerate(pairs):
            keys = pair[:, kv_head * head_dim : (kv_head + 1) * head_dim]
            values = pair[:, (kv_heads + kv_head) * head_dim : (kv_heads + kv_head + 1) * head_dim]
            scores = dot_nt(queries, keys) * head_dim ** (-0.5)
            causal = key_pos_ref[slot : slot + 1, :] <= query_pos
            weights = jnp.where(causal, jnp.exp(scores), 0.0)
            totals = totals + jnp.sum(weights, axis=-1, keepdims=True)
            summed = summed + jnp.dot(weights.astype(BF), values, preferred_element_type=F32)
        outputs = summed / totals
        logs = jnp.log(totals)
        for group in range(groups):
            head = kv_head * groups + group
            at = slice(group * count, (group + 1) * count)
            out_ref[:, head * head_dim : (head + 1) * head_dim] = outputs[at].astype(BF)
            log_ref[:, head : head + 1] = logs[at]


def attend(queries, pairs, query_pos, key_pos, head_dim):
    heads = queries.shape[1] // head_dim
    shapes = [(queries.shape, BF), ((queries.shape[0], heads), F32)]
    kernel = functools.partial(attend_kernel, head_dim)
    return rows_call(kernel, shapes, queries, query_pos, key_pos, *pairs)


def attend_back_kernel(
    head_dim, query_ref, query_pos_ref, key_pos_ref, out_ref, log_ref, grad_ref, *refs
):
    slots = (len(refs) - 1) // 2
    pairs, query_grad_ref, pair_grads = refs[:slots], refs[slots], refs[slots + 1 :]
    count = query_ref.shape[0]
    scale = head_dim ** (-0.5)
    kv_heads = pairs[0].shape[1] // (2 * head_dim)
    groups = query_ref.shape[1] // (kv_heads * head_dim)
    query_pos = jnp.concatenate([query_pos_ref[...]] * groups, axis=0)
    for kv_head in range(kv_heads):
        first = kv_head * groups
        queries = stack_heads(query_ref, first, groups, head_dim)
        grads = stack_heads(grad_ref, first, groups, head_dim)
        outputs = stack_heads(out_ref, first, groups, head_dim)
        logs = jnp.concatenate(
            [log_ref[:, first + i : first + i + 1] for i in range(groups)], axis=0
        )
        deltas = jnp.sum(grads.astype(F32) * outputs.astype(F32), axis=-1, keepdims=True)
        query_grad = jnp.zeros((groups * count, head_dim), F32)
        key_at = slice(kv_head * head_dim, (kv_head + 1) * head_dim)
        value_at = slice((kv_heads + kv_head) * head_dim, (kv_heads + kv_head + 1) * head_dim)
        for slot in range(slots):
            keys, values = pairs[slot][:, key_at], pairs[slot][:, value_at]
            scores = dot_nt(queries, keys) * scale
            causal = key_pos_ref[slot : slot + 1, :] <= query_pos
            probs = jnp.where(causal, jnp.exp(scores - logs), 0.0)
            value_grad = dot_tn(probs.astype(BF), grads)
            grad_probs = dot_nt(grads, values)
            grad_scores = (probs * (grad_probs - deltas) * scale).astype(BF)
            query_grad = query_grad + jnp.dot(grad_scores, keys, preferred_element_type=F32)
            key_grad = dot_tn(grad_scores, queries)
            pair_grads[slot][:, key_at] = key_grad.astype(pair_grads[slot].dtype)
            pair_grads[slot][:, value_at] = value_grad.astype(pair_grads[slot].dtype)
        for group in range(groups):
            head = first + group
            query_grad_ref[:, head * head_dim : (head + 1) * head_dim] = query_grad[
                group * count : (group + 1) * count
            ]


def attend_back(queries, pairs, query_pos, key_pos, outputs, logs, grads, head_dim):
    kernel = functools.partial(attend_back_kernel, head_dim)
    shapes = [(queries.shape, F32)]
    shapes += [(pair.shape, BF if slot else F32) for slot, pair in enumerate(pairs)]
    query_grad, *pair_grads = rows_call(
        kernel, shapes, queries, query_pos, key_pos, outputs, logs, grads, *pairs
    )
    return query_grad, pair_grads


class Links:
    def __init__(self, contexts, tensors):
        self.contexts, self.tensors = contexts, tensors
        self.count = contexts * tensors
        self.half = contexts // 2
        self.far_half = self.half * tensors
        self.half_groups = [
            [(part * self.half + member) * tensors + tensor for member in range(self.half)]
            for part in range(2)
            for tensor in range(tensors)
        ]
        self.context = lax.axis_index(CONTEXT)
        self.upper = self.context >= self.half
        self.place = self.context % self.half

    def swap(self, value, mask):
        return lax.ppermute(value, AXES, [(i, i ^ mask) for i in range(self.count)])

    def line_masks(self):
        return [2 * place * self.tensors for place in range(self.half)]

    def square_masks(self):
        return [
            side * self.tensors + row * 2 for side in range(2) for row in range(self.tensors // 2)
        ]

    def half_masks(self):
        return [member * self.tensors for member in range(self.half)]

    def by_part(self, mine, theirs):
        return jnp.where(self.upper, theirs, mine), jnp.where(self.upper, mine, theirs)

    def spread(self, value, masks):
        return [value] + [self.swap(value, mask) for mask in masks[1:]]

    def collect(self, chunks, masks):
        return self.total(self.fetch(chunks, masks))

    def fetch(self, chunks, masks):
        return [chunks[0]] + [
            self.swap(chunk.astype(BF), mask) for chunk, mask in zip(chunks[1:], masks[1:])
        ]

    def total(self, pieces):
        total = pieces[0].astype(F32)
        for piece in pieces[1:]:
            total = total + piece.astype(F32)
        return total

    def exchange_context(self, chunks):
        return lax.all_to_all(chunks, CONTEXT, 0, 0)

    def spread_context(self, value):
        return self.exchange_context(
            jnp.broadcast_to(value[None], (self.contexts, *value.shape))
        )

    def relative(self, slots, index):
        count, shape = slots.shape[0], slots.shape[1:]
        bit = 1
        while bit < count:
            pairs = slots.reshape(count // (2 * bit), 2, bit, *shape)
            flipped = jnp.concatenate([pairs[:, 1:], pairs[:, :1]], axis=1)
            odd = (index // bit) % 2 == 1
            slots = jnp.where(odd, flipped, pairs).reshape(count, *shape)
            bit *= 2
        return slots

    def gather_rows(self, rows):
        return self.gather_square(self.gather_line(rows))

    def gather_line(self, rows):
        return join(self.spread(rows, self.line_masks()))

    def gather_square(self, line):
        own = join(self.spread(line, self.square_masks()))
        return own, self.swap(own, 1)

    def move_start(self, chunks):
        return self.exchange_context(chunks)

    def reduce_start(self, own, other):
        other = self.swap(other.astype(BF), 1)
        half = lax.optimization_barrier(own.astype(BF)).astype(F32) + other.astype(F32)
        masks = self.square_masks()
        return self.fetch(jnp.split(half, len(masks), axis=0), masks)

    def reduce_end(self, pieces):
        line = self.total(pieces)
        masks = self.line_masks()
        return self.collect(jnp.split(line, len(masks), axis=0), masks)

    def reduce_rows(self, own, other):
        return self.reduce_end(self.reduce_start(own, other))

    def spread_rows(self, rows):
        for mask in (self.far_half, 2, 1):
            rows = join([rows, self.swap(rows, mask)])
        return rows

    def return_rows(self, partial):
        for mask in (1, 2, self.far_half):
            own, other = jnp.split(partial, 2, axis=0)
            partial = own + self.swap(other.astype(BF), mask).astype(F32)
        return partial

    def both_parts(self, mine, theirs):
        got = self.swap(theirs, self.far_half)
        joined = join_at([mine[None], got[None]], self.upper.astype(jnp.int32))
        return joined.reshape(2, *mine.shape)

    def gather_half(self, shard, behind):
        if not behind and self.half <= 4:
            return join_at(self.spread(shard, self.half_masks()), self.place)
        return lax.all_gather(
            shard, AXES, axis=1, tiled=True, axis_index_groups=self.half_groups
        )

    def scatter_start(self, partial):
        rows, columns = partial.shape
        partial = partial.reshape(2, rows // 2, columns)
        if self.half > 4:
            return [
                lax.psum_scatter(
                    partial.astype(BF),
                    AXES,
                    scatter_dimension=1,
                    axis_index_groups=self.half_groups,
                    tiled=True,
                )
            ]
        return self.fetch(split_at(partial, self.half, self.place), self.half_masks())

    def scatter_end(self, pieces):
        shard = self.total(pieces).astype(BF)
        mine = jnp.where(self.upper, shard[1], shard[0])
        theirs = jnp.where(self.upper, shard[0], shard[1])
        got = self.swap(theirs, self.far_half)
        return [part.astype(F32) for part in self.by_part(mine, got)]


def body(
    residual_in,
    grad_output,
    block_order,
    w_query,
    key_weight,
    value_weight,
    w_out,
    w_gate,
    w_up,
    w_down,
    attn_gain,
    mlp_gain,
    query_gain,
    key_gain,
):
    contexts, tensors = lax.axis_size(CONTEXT), lax.axis_size(TENSOR)
    links = Links(contexts, tensors)
    masks = links.half_masks()
    layers = w_query.shape[0]
    head_dim = query_gain.shape[1]
    local_rows, width = residual_in.shape
    context_rows = local_rows * tensors
    rows_per_block = context_rows // 2
    all_rows = context_rows * contexts
    key_pos = row_positions(block_order, jnp.int32(0), all_rows, rows_per_block)
    key_pos = links.relative(key_pos.reshape(contexts, context_rows), links.context)
    key_pos = key_pos.reshape(contexts, tensors, local_rows)
    tensor = lax.axis_index(TENSOR)
    key_pos = links.relative(key_pos.transpose(1, 0, 2), tensor)
    key_pos = key_pos.reshape(2, 2, 2, links.half, local_rows).transpose(3, 1, 0, 2, 4)
    key_pos = key_pos.reshape(links.half, 2 * context_rows)
    query_pos = key_pos[0]
    cosine, sine = rotary_tables(query_pos, head_dim)
    tables = (
        jnp.concatenate([cosine, cosine], axis=1),
        jnp.concatenate([-sine, sine], axis=1),
    )
    query_pos = query_pos[:, None]
    query_width, kv_width = w_query.shape[2] // 2, key_weight.shape[2] // 2
    query_heads = query_width // head_dim
    kv_heads = kv_width // head_dim
    units = w_gate.shape[2] // contexts
    shard = w_query.shape[1]
    query_gains = [query_gain[layer][None] for layer in range(layers)]
    key_gains = [key_gain[layer][None] for layer in range(layers)]

    gains = jnp.concatenate([attn_gain, mlp_gain], axis=0)
    gains = links.spread_context(gains).transpose(1, 0, 2).reshape(2 * layers, width)
    gains = gains.astype(F32)

    def ffn_parts(layer):
        parts = pack(w_gate, w_up, layer, contexts, 1 if layer else 2)
        return [*parts, w_down[layer].reshape(contexts, units, shard)]

    packed = []
    for layer in range(layers):
        packed.append(ffn_parts(layer))
    attn_weights, out_weights = [], []
    ffn_weights = [[] for _ in range(layers)]

    def fetch(layer):
        at = len(ffn_weights[layer])
        piece = links.move_start(packed[layer][at])
        ffn_weights[layer].append(piece)

    fetch(0)
    for layer in range(layers):
        parts = []
        for part in range(2):
            query_at = slice(part * query_width, (part + 1) * query_width)
            kv_at = slice(part * kv_width, (part + 1) * kv_width)
            columns = [
                w_query[layer][:, query_at],
                key_weight[layer][:, kv_at],
                value_weight[layer][:, kv_at],
                w_out[layer].T[:, query_at],
            ]
            parts.append(jnp.concatenate(columns, axis=1))
        mine, theirs = links.by_part(*parts)
        cuts = [query_width, query_width + 2 * kv_width] if layer else [query_width + 2 * kv_width]
        mine, theirs = jnp.split(mine, cuts, axis=1), jnp.split(theirs, cuts, axis=1)
        if layer:
            held = [links.both_parts(a, b) for a, b in zip(mine, theirs)]
        else:
            taken = links.both_parts(mine[0], theirs[0])
            taken = links.gather_half(taken, False)
            attn_weights.append(taken.reshape(width, -1))
        if not layer:
            taken = links.both_parts(mine[1], theirs[1])
            out_weights.append(links.gather_half(taken, False).reshape(width, -1))

    current = residual_in
    stored = []
    for layer in range(layers):
        gain_attn, gain_mlp = gains[layer], gains[layers + layer]
        normed_in = links.spread_rows(rms_scale(current, gain_attn).astype(BF))
        if layer:
            query_proj, pair_proj = [mm(normed_in, w) for w in attn_weights[layer]]
        else:
            projected = mm(normed_in, attn_weights[layer])
            query_proj, pair_proj = projected[:, :query_width], projected[:, query_width:]
        pairs = prep_heads(pair_proj, kv_heads, key_gains[layer], tables)
        pairs = links.spread(pairs, masks)
        queries = prep_heads(query_proj, query_heads, query_gains[layer], tables)
        if layer == 0:
            top_gradient = links.gather_rows(after(grad_output, *pairs).astype(BF))
        if layer == 0:
            out_weights.append(links.gather_half(held[2], True).reshape(width, -1))
        fetch(layer)
        output_rows, log_totals = attend(queries, pairs, query_pos, key_pos, head_dim)
        partial = mm_nt(output_rows, out_weights[layer])
        middle = current + links.return_rows(partial)
        line = links.gather_line(rms_scale(middle, gain_mlp).astype(BF))
        if layer == 0:
            fetch(0)
        normed_mid = links.gather_square(line)
        if layer + 1 < layers:
            fetch(layer + 1)
        inner, partial = [], []
        weights = ffn_weights[layer]
        *inner_parts, down = weights
        weights[:] = [jnp.concatenate(inner_parts, axis=1).reshape(width, 2 * units)]
        weights.append(down.transpose(1, 0, 2).reshape(units, width))
        for rows in normed_mid:
            both = mm(rows, weights[0])
            gate, up = both[:, :units], both[:, units:]
            hidden = (jax.nn.silu(gate) * up).astype(BF)
            inner.append((gate, up, hidden))
            partial.append(mm(hidden, weights[1]))
        if layer + 1 < layers:
            block_out = middle + links.reduce_rows(*partial)
            next_pairs = links.gather_half(held[1], True).reshape(width, -1)
            next_queries = links.gather_half(held[0], True).reshape(width, -1)
            attn_weights.append((next_queries, next_pairs))
        else:
            last = (middle, [half.astype(BF) for half in partial])
        stored.append(
            (
                current,
                normed_in,
                query_proj,
                pair_proj,
                queries,
                pairs,
                output_rows,
                log_totals,
                middle,
                normed_mid,
                inner,
            )
        )
        if layer + 1 < layers:
            current = block_out

    def finish_attn(left, late):
        out_pieces, *projected = after(left, late)
        d_out = jnp.concatenate(links.scatter_end(out_pieces), axis=1).T
        shards = [links.scatter_end(pieces) for pieces in projected]
        halves = [jnp.concatenate(pair, axis=1) for pair in zip(*shards)]
        cuts = [query_width, query_width + kv_width]
        d_query, d_key, d_value = [
            jnp.concatenate(pair, axis=1)
            for pair in zip(*[jnp.split(half, cuts, axis=1) for half in halves])
        ]
        return d_query, d_key, d_value, d_out

    grad_res, moved = grad_output, None
    weight_grads, gain_grads = [None] * layers, [None] * layers
    for layer in reversed(range(layers)):
        (
            layer_in,
            normed_in,
            query_proj,
            pair_proj,
            queries,
            pairs,
            output_rows,
            log_totals,
            middle,
            normed_mid,
            inner,
        ) = stored[layer]
        gain_attn, gain_mlp = gains[layer], gains[layers + layer]
        if layer + 1 == layers:
            grad_all = top_gradient
        else:
            line = links.gather_line(grad_res.astype(BF))
            grad_all = links.gather_square(line)
            final_pieces = after(final_pieces, line)
            final_out = middle_last + links.reduce_end(final_pieces)
            weight_grads[layer + 1] = finish_attn(left, line)
        partial, d_in, d_down = [], 0.0, 0.0
        weights = ffn_weights[layer]
        for rows, grad_rows, (gate, up, hidden) in zip(normed_mid, grad_all, inner):
            grad_hidden = mm_nt(grad_rows, weights[1])
            sigmoid = jax.nn.sigmoid(gate)
            grad_up = (grad_hidden * gate * sigmoid).astype(BF)
            grad_gate = (
                grad_hidden * up * sigmoid * (1.0 + gate * (1.0 - sigmoid))
            ).astype(BF)
            both = jnp.concatenate([grad_gate, grad_up], axis=1)
            partial.append(mm_nt(both, weights[0]))
            d_in = d_in + mm_tn(rows, both)
            d_down = d_down + mm_tn(hidden, grad_rows)
        held_grads = d_in.astype(BF).reshape(contexts, shard, 2 * units)
        down_grads = d_down.astype(BF).reshape(units, contexts, shard).transpose(1, 0, 2)
        last_moved, moved = moved, [None] * 2
        pieces = links.reduce_start(*partial)
        moved[1] = links.move_start(down_grads)
        grad_normed_mid = links.reduce_end(pieces)
        unused, norm_back = jax.vjp(rms_scale, middle, gain_mlp)
        grad_mid_part, d_mlp_gain = norm_back(grad_normed_mid)
        grad_mid = grad_res + grad_mid_part
        grad_mid_all = links.spread_rows(grad_mid.astype(BF))
        moved[0] = links.move_start(held_grads)
        out_pieces = links.scatter_start(mm_tn(grad_mid_all, output_rows))
        attention_gradient = mm(grad_mid_all, out_weights[layer]).astype(BF)
        if layer + 1 == layers:
            middle_last, partial_last = last
            final_pieces = links.reduce_start(*after(partial_last, grad_mid_all))
        query_grad, pair_grads = attend_back(
            queries,
            pairs,
            query_pos,
            key_pos,
            output_rows,
            log_totals,
            attention_gradient,
            head_dim,
        )
        pair_grads = [pair_grads[0]] + [
            links.swap(grad, mask) for grad, mask in zip(pair_grads[1:], masks[1:])
        ]
        grad_queries, d_query_gain = prep_heads_back(
            query_proj, query_heads, query_gains[layer], tables, [query_grad]
        )
        grad_pairs, d_key_gain = prep_heads_back(
            pair_proj, kv_heads, key_gains[layer], tables, pair_grads
        )
        if layer:
            partial = mm_nt(grad_queries, attn_weights[layer][0])
            partial = partial + mm_nt(grad_pairs, attn_weights[layer][1])
        else:
            grad_projected = jnp.concatenate([grad_queries, grad_pairs], axis=1)
            partial = mm_nt(grad_projected, attn_weights[layer])
        grad_normed_in = links.return_rows(partial)
        unused, input_back = jax.vjp(rms_scale, layer_in, gain_attn)
        grad_in_part, d_attn_gain = input_back(grad_normed_in)
        grad_res = grad_mid + grad_in_part
        projected = []
        for grads in (grad_queries, grad_pairs):
            projected.append(links.scatter_start(mm_tn(normed_in, grads)))
        left = (out_pieces, *projected)
        if layer == 0:
            weight_grads[0] = finish_attn(left, grad_res)
            every = after((moved, last_moved), partial)
            d_gate, d_up = unpack([piece[0] for piece in every])
            d_down = [piece[1].reshape(contexts * units, shard) for piece in every]
            d_down = jnp.stack(d_down).astype(F32)
        gain_grads[layer] = (d_attn_gain, d_mlp_gain, d_query_gain[0], d_key_gain[0])

    wide = jnp.stack([g[0] for g in gain_grads] + [g[1] for g in gain_grads])
    wide = wide.reshape(2 * layers, contexts, shard).transpose(1, 0, 2)
    narrow = jnp.stack([g[2] for g in gain_grads] + [g[3] for g in gain_grads])
    wide = wide.reshape(contexts, 1, 2 * layers * shard)
    narrow = jnp.broadcast_to(
        narrow.reshape(1, 1, 2 * layers * head_dim), (contexts, 1, 2 * layers * head_dim)
    )
    pieces = jnp.concatenate([wide, narrow], axis=2)
    pieces = jnp.broadcast_to(pieces, (contexts, tensors, pieces.shape[2]))
    pieces = pieces.reshape(contexts * tensors, -1)
    sums = jnp.sum(lax.all_to_all(pieces, AXES, 0, 0, tiled=True), axis=0)
    wide = sums[: 2 * layers * shard].reshape(2, layers, shard)
    narrow = sums[2 * layers * shard :].reshape(2, layers, head_dim)
    stacked = []
    for member in range(4):
        stacked.append(jnp.stack([grads[member] for grads in weight_grads]))
    stacked.extend((d_gate, d_up, d_down))
    return (final_out, grad_res, *stacked, wide[0], wide[1], narrow[0], narrow[1])


def solution(mesh):
    rows = P(AXES, None)
    in_split = P(None, CONTEXT, TENSOR)
    out_split = P(None, TENSOR, CONTEXT)
    gain = P(None, CONTEXT)
    weights = (in_split, in_split, in_split, out_split, in_split, in_split, out_split)
    return jax.shard_map(
        body,
        mesh=mesh,
        in_specs=(rows, rows, P(), *weights, gain, gain, P(), P()),
        out_specs=(rows, rows, *weights, gain, gain, P(), P()),
        check_vma=False,
    )
```

```python
import functools

import jax
import jax.numpy as jnp
from jax import lax
from jax.experimental import pallas as pl
from jax.experimental.pallas import tpu as pltpu
from jax.sharding import PartitionSpec as P

EPSILON = 1e-06
THETA = 1000000.0
CONTEXT, TENSOR = AXES = ("context", "tensor")
BF = jnp.bfloat16
F32 = jnp.float32


def mm(a, b):
    return jnp.dot(a, b, preferred_element_type=F32)


def mm_tn(a, b):
    return lax.dot_general(a, b, (((0,), (0,)), ((), ())), preferred_element_type=F32)


def mm_nt(a, b):
    return lax.dot_general(a, b, (((1,), (1,)), ((), ())), preferred_element_type=F32)


def rms_scale(row_data, gain_row):
    mean_square = jnp.mean(row_data * row_data, axis=-1, keepdims=True)
    return row_data * lax.rsqrt(mean_square + EPSILON) * gain_row


def rotary_tables(positions, head_dim):
    half_dim = head_dim // 2
    exponent = jnp.arange(half_dim, dtype=F32) * (2.0 / head_dim)
    inverse = jnp.power(F32(THETA), -exponent)
    angles = positions.astype(F32)[:, None] * inverse[None, :]
    return (jnp.cos(angles), jnp.sin(angles))


def row_positions(block_order, first_row, row_count, rows_per_block):
    rows_index = first_row + jnp.arange(row_count, dtype=jnp.int32)
    slot_index = rows_index // rows_per_block
    slots = jnp.arange(block_order.shape[0], dtype=jnp.int32)
    matches = slot_index[:, None] == slots[None, :]
    owners = jnp.sum(jnp.where(matches, block_order[None, :], 0), axis=1)
    return owners * rows_per_block + rows_index % rows_per_block


def after(value, *others):
    return lax.optimization_barrier((value, others))[0]


def rows_call(kernel, out_shapes, *operands):
    return pl.pallas_call(
        kernel,
        out_shape=[jax.ShapeDtypeStruct(shape, kind) for shape, kind in out_shapes],
        compiler_params=pltpu.CompilerParams(vmem_limit_bytes=48 * 1024 * 1024),
    )(*operands)


def join_kernel(*refs):
    *pieces, out_ref = refs
    count = pieces[0].shape[0]
    for slot, piece in enumerate(pieces):
        out_ref[slot * count : (slot + 1) * count, :] = piece[...]


def join(pieces):
    rows, width = pieces[0].shape
    return rows_call(join_kernel, [((len(pieces) * rows, width), pieces[0].dtype)], *pieces)[0]


def index_call(kernel, out_shapes, index, *operands):
    vmem = pl.BlockSpec(memory_space=pltpu.VMEM)
    return pl.pallas_call(
        kernel,
        in_specs=[pl.BlockSpec(memory_space=pltpu.SMEM)] + [vmem] * len(operands),
        out_specs=[vmem] * len(out_shapes),
        out_shape=[jax.ShapeDtypeStruct(shape, kind) for shape, kind in out_shapes],
        compiler_params=pltpu.CompilerParams(vmem_limit_bytes=48 * 1024 * 1024),
    )(index.reshape(1), *operands)


def join_at_kernel(index_ref, *refs):
    *pieces, out_ref = refs
    count = pieces[0].shape[1]
    for slot, piece in enumerate(pieces):
        first = pl.multiple_of((index_ref[0] ^ slot) * count, count)
        out_ref[:, pl.ds(first, count), :] = piece[...]


def join_at(pieces, index):
    parts, rows, width = pieces[0].shape
    shape = (parts, len(pieces) * rows, width)
    return index_call(join_at_kernel, [(shape, pieces[0].dtype)], index, *pieces)[0]


def split_at_kernel(index_ref, x_ref, *outs):
    count = outs[0].shape[1]
    for slot, out in enumerate(outs):
        first = pl.multiple_of((index_ref[0] ^ slot) * count, count)
        out[...] = x_ref[:, pl.ds(first, count), :].astype(out.dtype)


def split_at(x, places, index, own=F32):
    parts, rows, width = x.shape
    shape = (parts, rows // places, width)
    shapes = [(shape, BF if slot else own) for slot in range(places)]
    return index_call(split_at_kernel, shapes, index, x)


def pack_kernel(layer, gate_ref, up_ref, *outs):
    slots, rows, width = outs[0].shape
    units = width // 2
    for part, out in enumerate(outs):
        row_at = slice(part * rows, (part + 1) * rows)
        gate = gate_ref[layer, row_at, :].astype(F32)
        up = up_ref[layer, row_at, :].astype(F32)
        for slot in range(slots):
            at = slice(slot * units, (slot + 1) * units)
            out[slot, :, :units] = gate[:, at].astype(BF)
            out[slot, :, units:] = up[:, at].astype(BF)


def pack(w_gate, w_up, layer, slots, parts):
    rows, columns = w_gate.shape[1:]
    shapes = [((slots, rows // parts, 2 * columns // slots), BF)] * parts
    return rows_call(functools.partial(pack_kernel, layer), shapes, w_gate, w_up)


def unpack_kernel(*refs):
    *layers, gate_ref, up_ref = refs
    for layer, pieces in enumerate(layers):
        count, _, width = pieces.shape
        units = width // 2
        for slot in range(count):
            at = slice(slot * units, (slot + 1) * units)
            both = pieces[slot].astype(F32)
            gate_ref[layer, :, at] = both[:, :units]
            up_ref[layer, :, at] = both[:, units:]


def unpack(layers):
    count, rows, width = layers[0].shape
    shape = (len(layers), rows, count * width // 2)
    return rows_call(unpack_kernel, [(shape, F32)] * 2, *layers)


def prep_kernel(heads, x_ref, gain_ref, cos_ref, sin_ref, out_ref):
    head_dim = gain_ref.shape[1]
    for head in range(x_ref.shape[1] // head_dim):
        at = slice(head * head_dim, (head + 1) * head_dim)
        rows = x_ref[:, at]
        if head < heads:
            mean_square = jnp.mean(rows * rows, axis=-1, keepdims=True)
            rows = rows * lax.rsqrt(mean_square + EPSILON) * gain_ref[...]
            rows = rows * cos_ref[...] + pltpu.roll(rows, head_dim // 2, 1) * sin_ref[...]
        out_ref[:, at] = rows.astype(BF)


def prep_heads(projected, heads, gain, tables):
    kernel = functools.partial(prep_kernel, heads)
    return rows_call(kernel, [(projected.shape, BF)], projected, gain, *tables)[0]


def prep_back_kernel(heads, x_ref, gain_ref, cos_ref, sin_ref, *refs):
    grads, (out_ref, gain_grad_ref) = refs[:-2], refs[-2:]
    head_dim = gain_ref.shape[1]
    gain_grad = jnp.zeros((1, head_dim), F32)
    for head in range(x_ref.shape[1] // head_dim):
        at = slice(head * head_dim, (head + 1) * head_dim)
        grad = grads[0][:, at].astype(F32)
        for piece in grads[1:]:
            grad = grad + piece[:, at].astype(F32)
        if head < heads:
            rows = x_ref[:, at]
            mean_square = jnp.mean(rows * rows, axis=-1, keepdims=True)
            scale = lax.rsqrt(mean_square + EPSILON)
            unit = rows * scale
            grad = grad * cos_ref[...] + pltpu.roll(grad * sin_ref[...], head_dim // 2, 1)
            gain_grad = gain_grad + jnp.sum(grad * unit, axis=0, keepdims=True)
            grad = grad * gain_ref[...]
            grad = scale * (grad - unit * jnp.mean(grad * unit, axis=-1, keepdims=True))
        out_ref[:, at] = grad.astype(BF)
    gain_grad_ref[...] = gain_grad


def prep_heads_back(projected, heads, gain, tables, grads):
    kernel = functools.partial(prep_back_kernel, heads)
    shapes = [(projected.shape, BF), (gain.shape, F32)]
    return rows_call(kernel, shapes, projected, gain, *tables, *grads)


def dot_nt(a, b):
    return lax.dot_general(a, b, (((1,), (1,)), ((), ())), preferred_element_type=F32)


def dot_tn(a, b):
    return lax.dot_general(a, b, (((0,), (0,)), ((), ())), preferred_element_type=F32)


def stack_heads(ref, first, groups, head_dim):
    return jnp.concatenate(
        [ref[:, (first + i) * head_dim : (first + i + 1) * head_dim] for i in range(groups)], axis=0
    )


def attend_kernel(head_dim, query_ref, query_pos_ref, key_pos_ref, *refs):
    pairs, (out_ref, log_ref) = refs[:-2], refs[-2:]
    count = query_ref.shape[0]
    kv_heads = pairs[0].shape[1] // (2 * head_dim)
    groups = query_ref.shape[1] // (kv_heads * head_dim)
    query_pos = jnp.concatenate([query_pos_ref[...]] * groups, axis=0)
    for kv_head in range(kv_heads):
        queries = stack_heads(query_ref, kv_head * groups, groups, head_dim)
        totals = jnp.zeros((groups * count, 1), F32)
        summed = jnp.zeros((groups * count, head_dim), F32)
        for slot, pair in enumerate(pairs):
            keys = pair[:, kv_head * head_dim : (kv_head + 1) * head_dim]
            values = pair[:, (kv_heads + kv_head) * head_dim : (kv_heads + kv_head + 1) * head_dim]
            scores = dot_nt(queries, keys) * head_dim ** (-0.5)
            causal = key_pos_ref[slot : slot + 1, :] <= query_pos
            weights = jnp.where(causal, jnp.exp(scores), 0.0)
            totals = totals + jnp.sum(weights, axis=-1, keepdims=True)
            summed = summed + jnp.dot(weights.astype(BF), values, preferred_element_type=F32)
        outputs = summed / totals
        logs = jnp.log(totals)
        for group in range(groups):
            head = kv_head * groups + group
            at = slice(group * count, (group + 1) * count)
            out_ref[:, head * head_dim : (head + 1) * head_dim] = outputs[at].astype(BF)
            log_ref[:, head : head + 1] = logs[at]


def attend(queries, pairs, query_pos, key_pos, head_dim):
    heads = queries.shape[1] // head_dim
    shapes = [(queries.shape, BF), ((queries.shape[0], heads), F32)]
    kernel = functools.partial(attend_kernel, head_dim)
    return rows_call(kernel, shapes, queries, query_pos, key_pos, *pairs)


def attend_back_kernel(
    head_dim, query_ref, query_pos_ref, key_pos_ref, out_ref, log_ref, grad_ref, *refs
):
    slots = (len(refs) - 1) // 2
    pairs, query_grad_ref, pair_grads = refs[:slots], refs[slots], refs[slots + 1 :]
    count = query_ref.shape[0]
    scale = head_dim ** (-0.5)
    kv_heads = pairs[0].shape[1] // (2 * head_dim)
    groups = query_ref.shape[1] // (kv_heads * head_dim)
    query_pos = jnp.concatenate([query_pos_ref[...]] * groups, axis=0)
    for kv_head in range(kv_heads):
        first = kv_head * groups
        queries = stack_heads(query_ref, first, groups, head_dim)
        grads = stack_heads(grad_ref, first, groups, head_dim)
        outputs = stack_heads(out_ref, first, groups, head_dim)
        logs = jnp.concatenate(
            [log_ref[:, first + i : first + i + 1] for i in range(groups)], axis=0
        )
        deltas = jnp.sum(grads.astype(F32) * outputs.astype(F32), axis=-1, keepdims=True)
        query_grad = jnp.zeros((groups * count, head_dim), F32)
        key_at = slice(kv_head * head_dim, (kv_head + 1) * head_dim)
        value_at = slice((kv_heads + kv_head) * head_dim, (kv_heads + kv_head + 1) * head_dim)
        for slot in range(slots):
            keys, values = pairs[slot][:, key_at], pairs[slot][:, value_at]
            scores = dot_nt(queries, keys) * scale
            causal = key_pos_ref[slot : slot + 1, :] <= query_pos
            probs = jnp.where(causal, jnp.exp(scores - logs), 0.0)
            value_grad = dot_tn(probs.astype(BF), grads)
            grad_probs = dot_nt(grads, values)
            grad_scores = (probs * (grad_probs - deltas) * scale).astype(BF)
            query_grad = query_grad + jnp.dot(grad_scores, keys, preferred_element_type=F32)
            key_grad = dot_tn(grad_scores, queries)
            pair_grads[slot][:, key_at] = key_grad.astype(pair_grads[slot].dtype)
            pair_grads[slot][:, value_at] = value_grad.astype(pair_grads[slot].dtype)
        for group in range(groups):
            head = first + group
            query_grad_ref[:, head * head_dim : (head + 1) * head_dim] = query_grad[
                group * count : (group + 1) * count
            ]


def attend_back(queries, pairs, query_pos, key_pos, outputs, logs, grads, head_dim):
    kernel = functools.partial(attend_back_kernel, head_dim)
    shapes = [(queries.shape, F32)]
    shapes += [(pair.shape, BF if slot else F32) for slot, pair in enumerate(pairs)]
    query_grad, *pair_grads = rows_call(
        kernel, shapes, queries, query_pos, key_pos, outputs, logs, grads, *pairs
    )
    return query_grad, pair_grads


class Links:
    def __init__(self, contexts, tensors):
        self.contexts, self.tensors = contexts, tensors
        self.count = contexts * tensors
        self.half = contexts // 2
        self.far_half = self.half * tensors
        self.half_groups = [
            [(part * self.half + member) * tensors + tensor for member in range(self.half)]
            for part in range(2)
            for tensor in range(tensors)
        ]
        self.context = lax.axis_index(CONTEXT)
        self.upper = self.context >= self.half
        self.place = self.context % self.half

    def swap(self, value, mask):
        return lax.ppermute(value, AXES, [(i, i ^ mask) for i in range(self.count)])

    def line_masks(self):
        return [2 * place * self.tensors for place in range(self.half)]

    def square_masks(self):
        return [
            side * self.tensors + row * 2 for side in range(2) for row in range(self.tensors // 2)
        ]

    def half_masks(self):
        return [member * self.tensors for member in range(self.half)]

    def by_part(self, mine, theirs):
        return jnp.where(self.upper, theirs, mine), jnp.where(self.upper, mine, theirs)

    def spread(self, value, masks):
        return [value] + [self.swap(value, mask) for mask in masks[1:]]

    def collect(self, chunks, masks):
        return self.total(self.fetch(chunks, masks))

    def fetch(self, chunks, masks):
        return [chunks[0]] + [
            self.swap(chunk.astype(BF), mask) for chunk, mask in zip(chunks[1:], masks[1:])
        ]

    def total(self, pieces):
        total = pieces[0].astype(F32)
        for piece in pieces[1:]:
            total = total + piece.astype(F32)
        return total

    def exchange_context(self, chunks):
        return lax.all_to_all(chunks, CONTEXT, 0, 0)

    def spread_context(self, value):
        return self.exchange_context(
            jnp.broadcast_to(value[None], (self.contexts, *value.shape))
        )

    def relative(self, slots, index):
        count, shape = slots.shape[0], slots.shape[1:]
        bit = 1
        while bit < count:
            pairs = slots.reshape(count // (2 * bit), 2, bit, *shape)
            flipped = jnp.concatenate([pairs[:, 1:], pairs[:, :1]], axis=1)
            odd = (index // bit) % 2 == 1
            slots = jnp.where(odd, flipped, pairs).reshape(count, *shape)
            bit *= 2
        return slots

    def gather_rows(self, rows):
        return self.gather_square(self.gather_line(rows))

    def gather_line(self, rows):
        return join(self.spread(rows, self.line_masks()))

    def gather_square(self, line):
        own = join(self.spread(line, self.square_masks()))
        return own, self.swap(own, 1)

    def move_start(self, chunks):
        return self.exchange_context(chunks)

    def reduce_start(self, own, other):
        other = self.swap(other.astype(BF), 1)
        half = lax.optimization_barrier(own.astype(BF)).astype(F32) + other.astype(F32)
        masks = self.square_masks()
        return self.fetch(jnp.split(half, len(masks), axis=0), masks)

    def reduce_end(self, pieces):
        line = self.total(pieces)
        masks = self.line_masks()
        return self.collect(jnp.split(line, len(masks), axis=0), masks)

    def reduce_rows(self, own, other):
        return self.reduce_end(self.reduce_start(own, other))

    def spread_rows(self, rows):
        for mask in (self.far_half, 2, 1):
            rows = join([rows, self.swap(rows, mask)])
        return rows

    def return_rows(self, partial):
        for mask in (1, 2, self.far_half):
            own, other = jnp.split(partial, 2, axis=0)
            partial = own + self.swap(other.astype(BF), mask).astype(F32)
        return partial

    def both_parts(self, mine, theirs):
        got = self.swap(theirs, self.far_half)
        joined = join_at([mine[None], got[None]], self.upper.astype(jnp.int32))
        return joined.reshape(2, *mine.shape)

    def gather_half(self, shard, behind):
        if not behind and self.half <= 4:
            return join_at(self.spread(shard, self.half_masks()), self.place)
        return lax.all_gather(
            shard, AXES, axis=1, tiled=True, axis_index_groups=self.half_groups
        )

    def scatter_start(self, partial):
        rows, columns = partial.shape
        partial = partial.reshape(2, rows // 2, columns)
        if self.half > 4:
            return [
                lax.psum_scatter(
                    partial.astype(BF),
                    AXES,
                    scatter_dimension=1,
                    axis_index_groups=self.half_groups,
                    tiled=True,
                )
            ]
        return self.fetch(split_at(partial, self.half, self.place), self.half_masks())

    def scatter_end(self, pieces):
        shard = self.total(pieces).astype(BF)
        mine = jnp.where(self.upper, shard[1], shard[0])
        theirs = jnp.where(self.upper, shard[0], shard[1])
        got = self.swap(theirs, self.far_half)
        return [part.astype(F32) for part in self.by_part(mine, got)]


def body(
    residual_in,
    grad_output,
    block_order,
    w_query,
    key_weight,
    value_weight,
    w_out,
    w_gate,
    w_up,
    w_down,
    attn_gain,
    mlp_gain,
    query_gain,
    key_gain,
):
    contexts, tensors = lax.axis_size(CONTEXT), lax.axis_size(TENSOR)
    links = Links(contexts, tensors)
    masks = links.half_masks()
    layers = w_query.shape[0]
    head_dim = query_gain.shape[1]
    local_rows, width = residual_in.shape
    context_rows = local_rows * tensors
    rows_per_block = context_rows // 2
    all_rows = context_rows * contexts
    key_pos = row_positions(block_order, jnp.int32(0), all_rows, rows_per_block)
    key_pos = links.relative(key_pos.reshape(contexts, context_rows), links.context)
    key_pos = key_pos.reshape(contexts, tensors, local_rows)
    tensor = lax.axis_index(TENSOR)
    key_pos = links.relative(key_pos.transpose(1, 0, 2), tensor)
    key_pos = key_pos.reshape(2, 2, 2, links.half, local_rows).transpose(3, 1, 0, 2, 4)
    key_pos = key_pos.reshape(links.half, 2 * context_rows)
    query_pos = key_pos[0]
    cosine, sine = rotary_tables(query_pos, head_dim)
    tables = (
        jnp.concatenate([cosine, cosine], axis=1),
        jnp.concatenate([-sine, sine], axis=1),
    )
    query_pos = query_pos[:, None]
    query_width, kv_width = w_query.shape[2] // 2, key_weight.shape[2] // 2
    query_heads = query_width // head_dim
    kv_heads = kv_width // head_dim
    units = w_gate.shape[2] // contexts
    shard = w_query.shape[1]
    query_gains = [query_gain[layer][None] for layer in range(layers)]
    key_gains = [key_gain[layer][None] for layer in range(layers)]

    gains = jnp.concatenate([attn_gain, mlp_gain], axis=0)
    gains = links.spread_context(gains).transpose(1, 0, 2).reshape(2 * layers, width)
    gains = gains.astype(F32)

    def ffn_parts(layer):
        parts = pack(w_gate, w_up, layer, contexts, 1 if layer else 2)
        return [*parts, w_down[layer].reshape(contexts, units, shard)]

    packed = []
    for layer in range(layers):
        packed.append(ffn_parts(layer))
    attn_weights, out_weights = [], []
    ffn_weights = [[] for _ in range(layers)]

    def fetch(layer):
        at = len(ffn_weights[layer])
        piece = links.move_start(packed[layer][at])
        ffn_weights[layer].append(piece)

    fetch(0)
    for layer in range(layers):
        parts = []
        for part in range(2):
            query_at = slice(part * query_width, (part + 1) * query_width)
            kv_at = slice(part * kv_width, (part + 1) * kv_width)
            columns = [
                w_query[layer][:, query_at],
                key_weight[layer][:, kv_at],
                value_weight[layer][:, kv_at],
                w_out[layer].T[:, query_at],
            ]
            parts.append(jnp.concatenate(columns, axis=1))
        mine, theirs = links.by_part(*parts)
        cuts = [query_width, query_width + 2 * kv_width] if layer else [query_width + 2 * kv_width]
        mine, theirs = jnp.split(mine, cuts, axis=1), jnp.split(theirs, cuts, axis=1)
        if layer:
            held = [links.both_parts(a, b) for a, b in zip(mine, theirs)]
        else:
            taken = links.both_parts(mine[0], theirs[0])
            taken = links.gather_half(taken, False)
            attn_weights.append(taken.reshape(width, -1))
        if not layer:
            taken = links.both_parts(mine[1], theirs[1])
            out_weights.append(links.gather_half(taken, False).reshape(width, -1))

    current = residual_in
    stored = []
    for layer in range(layers):
        gain_attn, gain_mlp = gains[layer], gains[layers + layer]
        normed_in = links.spread_rows(rms_scale(current, gain_attn).astype(BF))
        if layer:
            query_proj, pair_proj = [mm(normed_in, w) for w in attn_weights[layer]]
        else:
            projected = mm(normed_in, attn_weights[layer])
            query_proj, pair_proj = projected[:, :query_width], projected[:, query_width:]
        pairs = prep_heads(pair_proj, kv_heads, key_gains[layer], tables)
        pairs = links.spread(pairs, masks)
        queries = prep_heads(query_proj, query_heads, query_gains[layer], tables)
        if layer == 0:
            top_gradient = links.gather_rows(after(grad_output, *pairs).astype(BF))
        if layer == 0:
            out_weights.append(links.gather_half(held[2], True).reshape(width, -1))
        fetch(layer)
        output_rows, log_totals = attend(queries, pairs, query_pos, key_pos, head_dim)
        partial = mm_nt(output_rows, out_weights[layer])
        middle = current + links.return_rows(partial)
        line = links.gather_line(rms_scale(middle, gain_mlp).astype(BF))
        if layer == 0:
            fetch(0)
        normed_mid = links.gather_square(line)
        if layer + 1 < layers:
            fetch(layer + 1)
        inner, partial = [], []
        weights = ffn_weights[layer]
        *inner_parts, down = weights
        weights[:] = [jnp.concatenate(inner_parts, axis=1).reshape(width, 2 * units)]
        weights.append(down.transpose(1, 0, 2).reshape(units, width))
        for rows in normed_mid:
            both = mm(rows, weights[0])
            gate, up = both[:, :units], both[:, units:]
            hidden = (jax.nn.silu(gate) * up).astype(BF)
            inner.append((gate, up, hidden))
            partial.append(mm(hidden, weights[1]))
        if layer + 1 < layers:
            block_out = middle + links.reduce_rows(*partial)
            next_pairs = links.gather_half(held[1], True).reshape(width, -1)
            next_queries = links.gather_half(held[0], True).reshape(width, -1)
            attn_weights.append((next_queries, next_pairs))
        else:
            last = (middle, [half.astype(BF) for half in partial])
        stored.append(
            (
                current,
                normed_in,
                query_proj,
                pair_proj,
                queries,
                pairs,
                output_rows,
                log_totals,
                middle,
                normed_mid,
                inner,
            )
        )
        if layer + 1 < layers:
            current = block_out

    def finish_attn(left, late):
        (out_pieces,), projected = after(left[:1], late[0]), after(left[1:], late[1])
        d_out = jnp.concatenate(links.scatter_end(out_pieces), axis=1).T
        shards = [links.scatter_end(pieces) for pieces in projected]
        halves = [jnp.concatenate(pair, axis=1) for pair in zip(*shards)]
        cuts = [query_width, query_width + kv_width]
        d_query, d_key, d_value = [
            jnp.concatenate(pair, axis=1)
            for pair in zip(*[jnp.split(half, cuts, axis=1) for half in halves])
        ]
        return d_query, d_key, d_value, d_out

    grad_res, moved = grad_output, None
    weight_grads, gain_grads = [None] * layers, [None] * layers
    for layer in reversed(range(layers)):
        (
            layer_in,
            normed_in,
            query_proj,
            pair_proj,
            queries,
            pairs,
            output_rows,
            log_totals,
            middle,
            normed_mid,
            inner,
        ) = stored[layer]
        gain_attn, gain_mlp = gains[layer], gains[layers + layer]
        if layer + 1 == layers:
            grad_all = top_gradient
        else:
            line = links.gather_line(grad_res.astype(BF))
            grad_all = links.gather_square(line)
            final_pieces = after(final_pieces, line)
            final_out = middle_last + links.reduce_end(final_pieces)
            weight_grads[layer + 1] = finish_attn(left, (line, line))
        partial, d_in, d_down = [], 0.0, 0.0
        weights = ffn_weights[layer]
        for rows, grad_rows, (gate, up, hidden) in zip(normed_mid, grad_all, inner):
            grad_hidden = mm_nt(grad_rows, weights[1])
            sigmoid = jax.nn.sigmoid(gate)
            grad_up = (grad_hidden * gate * sigmoid).astype(BF)
            grad_gate = (
                grad_hidden * up * sigmoid * (1.0 + gate * (1.0 - sigmoid))
            ).astype(BF)
            both = jnp.concatenate([grad_gate, grad_up], axis=1)
            partial.append(mm_nt(both, weights[0]))
            d_in = d_in + mm_tn(rows, both)
            d_down = d_down + mm_tn(hidden, grad_rows)
        held_grads = d_in.astype(BF).reshape(contexts, shard, 2 * units)
        down_grads = d_down.astype(BF).reshape(units, contexts, shard).transpose(1, 0, 2)
        last_moved, moved = moved, [None] * 2
        pieces = links.reduce_start(*partial)
        moved[1] = links.move_start(down_grads)
        grad_normed_mid = links.reduce_end(pieces)
        unused, norm_back = jax.vjp(rms_scale, middle, gain_mlp)
        grad_mid_part, d_mlp_gain = norm_back(grad_normed_mid)
        grad_mid = grad_res + grad_mid_part
        grad_mid_all = links.spread_rows(grad_mid.astype(BF))
        moved[0] = links.move_start(held_grads)
        out_pieces = links.scatter_start(mm_tn(grad_mid_all, output_rows))
        attention_gradient = mm(grad_mid_all, out_weights[layer]).astype(BF)
        if layer + 1 == layers:
            middle_last, partial_last = last
            final_pieces = links.reduce_start(*after(partial_last, grad_mid_all))
        query_grad, pair_grads = attend_back(
            queries,
            pairs,
            query_pos,
            key_pos,
            output_rows,
            log_totals,
            attention_gradient,
            head_dim,
        )
        pair_grads = [pair_grads[0]] + [
            links.swap(grad, mask) for grad, mask in zip(pair_grads[1:], masks[1:])
        ]
        grad_queries, d_query_gain = prep_heads_back(
            query_proj, query_heads, query_gains[layer], tables, [query_grad]
        )
        grad_pairs, d_key_gain = prep_heads_back(
            pair_proj, kv_heads, key_gains[layer], tables, pair_grads
        )
        if layer:
            partial = mm_nt(grad_queries, attn_weights[layer][0])
            partial = partial + mm_nt(grad_pairs, attn_weights[layer][1])
        else:
            grad_projected = jnp.concatenate([grad_queries, grad_pairs], axis=1)
            partial = mm_nt(grad_projected, attn_weights[layer])
        grad_normed_in = links.return_rows(partial)
        unused, input_back = jax.vjp(rms_scale, layer_in, gain_attn)
        grad_in_part, d_attn_gain = input_back(grad_normed_in)
        grad_res = grad_mid + grad_in_part
        projected = []
        for grads in (grad_queries, grad_pairs):
            projected.append(links.scatter_start(mm_tn(normed_in, grads)))
        left = (out_pieces, *projected)
        if layer == 0:
            weight_grads[0] = finish_attn(left, (partial, grad_res))
            every = after((moved, last_moved), partial)
            d_gate, d_up = unpack([piece[0] for piece in every])
            d_down = [piece[1].reshape(contexts * units, shard) for piece in every]
            d_down = jnp.stack(d_down).astype(F32)
        gain_grads[layer] = (d_attn_gain, d_mlp_gain, d_query_gain[0], d_key_gain[0])

    wide = jnp.stack([g[0] for g in gain_grads] + [g[1] for g in gain_grads])
    wide = wide.reshape(2 * layers, contexts, shard).transpose(1, 0, 2)
    narrow = jnp.stack([g[2] for g in gain_grads] + [g[3] for g in gain_grads])
    wide = wide.reshape(contexts, 1, 2 * layers * shard)
    narrow = jnp.broadcast_to(
        narrow.reshape(1, 1, 2 * layers * head_dim), (contexts, 1, 2 * layers * head_dim)
    )
    pieces = jnp.concatenate([wide, narrow], axis=2)
    pieces = jnp.broadcast_to(pieces, (contexts, tensors, pieces.shape[2]))
    pieces = pieces.reshape(contexts * tensors, -1)
    sums = jnp.sum(lax.all_to_all(pieces, AXES, 0, 0, tiled=True), axis=0)
    wide = sums[: 2 * layers * shard].reshape(2, layers, shard)
    narrow = sums[2 * layers * shard :].reshape(2, layers, head_dim)
    stacked = []
    for member in range(4):
        stacked.append(jnp.stack([grads[member] for grads in weight_grads]))
    stacked.extend((d_gate, d_up, d_down))
    return (final_out, grad_res, *stacked, wide[0], wide[1], narrow[0], narrow[1])


def solution(mesh):
    rows = P(AXES, None)
    in_split = P(None, CONTEXT, TENSOR)
    out_split = P(None, TENSOR, CONTEXT)
    gain = P(None, CONTEXT)
    weights = (in_split, in_split, in_split, out_split, in_split, in_split, out_split)
    return jax.shard_map(
        body,
        mesh=mesh,
        in_specs=(rows, rows, P(), *weights, gain, gain, P(), P()),
        out_specs=(rows, rows, *weights, gain, gain, P(), P()),
        check_vma=False,
    )
```
